512 devices in a mesh: fsdp: 128 (over z, y, core), seq: 4 (over x).
Axes of the slice: x: 4, y: 8, z: 8, core: 2. Of those that a mesh axis runs over, the one named last changes fastest.
Arguments:
- text_embeds: bfloat16 [35840, 4096], P('fsdp'), may hold values from -8 to 8
- vision_tokens: bfloat16 [16384, 4096], P('fsdp', 'seq'), may hold values from -6 to 6
- vision_request: int32 [16384, 1], P('fsdp'), may hold values from 0 to 127; in each aligned block of 128 rows (0 to 127, 128 to 255, ...) at most 2 rows name the same one
- image_start: int32 [128], P('fsdp'), may hold values from 1 to 16
- lengths: int32 [128], P('fsdp'), may hold values from 273 to 280
- attn_gain: float32 [4096], replicated, may hold values from 0.5 to 1.5
- w_query: bfloat16 [4096, 2048], P('fsdp', 'seq'), may hold values from -1 to 1
- w_key: bfloat16 [4096, 2048], P('fsdp', 'seq'), may hold values from -1 to 1
- w_value: bfloat16 [4096, 2048], P('fsdp', 'seq'), may hold values from -0.09375 to 0.09375
- w_out: bfloat16 [2048, 4096], P(None, 'fsdp'), may hold values from -0.125 to 0.125
- final_gain: float32 [4096], replicated, may hold values from 0.25 to 1.75
- lm_head: bfloat16 [4096, 32000], P(None, 'fsdp'), may hold values from -0.25 to 0.25
Outputs:
- state_rms: float32 [128], P('seq')
- max_logit: float32 [128], P('seq')
The draws below stay inside these ranges and needn't reach their ends.
Inputs may be any that keep to these rules, and one draw needn't show every extreme that they name: `vision_request`: within the 128 vision tokens of one index of fsdp no request is named more than 2 times, a bound that some block reaches; every request is named by some vision token. `lengths`: each request's image tokens end before its last token.
All inputs are finite; a program needn't handle non-finite values.
Results may differ from the reference program's by a relative error of at most 0.0024.
Values may be sent and summed in bfloat16 or wider, within the bound.
No kernel may reach another device: no remote copies, remote signals or barrier semaphores. Data moves between devices by JAX's collectives and lax.ppermute only.
A program may use at most 128 MiB of HBM per device.

```python
import math
import jax
import jax.numpy as jnp
import numpy as np
from jax import lax

D = 4096
HD = 128
VOCAB = 32000
HEADS = 16
VT_GRP = 128
SEQ_LEN = 280
REQUESTS = 128
VTOK = 16384
CAP = 2
IMG_MAX = 256
ATTN = 2048


def column_scale():
    return 0.6 + 1.2 * jnp.arange(D, dtype=jnp.float32) / D


def draw_text_embeds(key, part):
    noise = jax.random.normal(jax.random.fold_in(key, 11), (REQUESTS * SEQ_LEN, D), jnp.float32)
    rows = noise
    return jnp.clip(rows * column_scale()[None, :], -8.0, 8.0).astype(jnp.bfloat16)


def draw_w_query(key, part):
    noise = jax.random.normal(jax.random.fold_in(key, 1), (D, HEADS * HD), jnp.float32) * math.sqrt(2.0 / D)
    weights = noise
    return jnp.clip(weights, -1.0, 1.0).astype(jnp.bfloat16)


def draw_w_key(key, part):
    noise = jax.random.normal(jax.random.fold_in(key, 2), (D, HEADS * HD), jnp.float32) * math.sqrt(2.0 / D)
    weights = noise
    return jnp.clip(weights, -1.0, 1.0).astype(jnp.bfloat16)


def with_ends(values, key, smallest, high):
    extent = values.shape
    index_at = [jax.random.randint(jax.random.fold_in(key, axis), (), 0, extent[axis]) for axis in range(len(extent))]
    values = values.at[tuple(index_at)].set(smallest)
    longest = extent.index(max(extent))
    index_at[longest] = (index_at[longest] + 1) % extent[longest]
    return values.at[tuple(index_at)].set(high)


def steps_of(key, shape, pieces, smallest, high):
    gain = 1.0
    for dim, parts in pieces:
        draws = jax.random.uniform(jax.random.fold_in(jax.random.fold_in(key, 6), dim), (parts,), jnp.float32, smallest / len(pieces), high / len(pieces))
        gain = gain * jnp.repeat(jnp.exp(draws), shape[dim] // parts).reshape((-1,) + (1,) * (len(shape) - 1 - dim))
    return gain


def deal_out(own_key, own, number, rows, amount, top, bound, lean):
    order = jax.random.permutation(own_key, amount)
    heavy_load, ordinary = load_shares(amount, rows * top, bound, lean, True), load_shares(amount, rows * top, bound, lean, False)
    places = jnp.arange(amount)

    def named(tallies, rotation):
        used = int((tallies > 0).sum())
        fixed = max(1, used // 4)
        moved = fixed + (places - fixed + rotation * (used - fixed)) % max(1, amount - fixed)
        return jnp.zeros((amount,), jnp.int32).at[order[jnp.where(places < fixed, places, moved)]].set(jnp.asarray(tallies, jnp.int32))

    tallies = jnp.where(number % 4 == 0, named(heavy_load, number // 4), named(ordinary, number - number // 4 - 1))
    mixed = jax.random.permutation(jax.random.fold_in(own, 3), amount)
    source_of, sink = mixed[0:amount // 2 * 2:2], mixed[1:amount // 2 * 2:2]
    margin = jnp.minimum(tallies[source_of] - 1, bound - tallies[sink]) // 2
    margin = jnp.where((source_of == order[0]) | (sink == order[0]) | (tallies[sink] == 0), 0, jnp.maximum(margin, 0))
    moved = jax.random.randint(jax.random.fold_in(own, 4), (amount // 2,), 0, 1 << 20) % (margin + 1)
    tallies = tallies.at[source_of].add(-moved).at[sink].add(moved)
    labels = jnp.searchsorted(jnp.cumsum(tallies), jnp.arange(rows * top), side="right").astype(jnp.int32)
    listing = labels.reshape(top, rows).T
    listing = listing[jax.random.permutation(jax.random.fold_in(own, 1), rows)]
    rotation = jax.random.randint(jax.random.fold_in(own, 2), (rows, 1), 0, top)
    return jnp.take_along_axis(listing, (jnp.arange(top)[None, :] + rotation) % top, axis=1)


def load_shares(number_of, total, bound, skew, full):
    loads = [(1 << 20) // math.isqrt(rank ** skew) + 1 for rank in range(1, number_of + 1)]
    largest = bound if full else min(bound, max(-(-total // number_of), total * loads[0] // sum(loads)))
    least = 1 if total - largest >= number_of - 1 else 0
    counts, surplus = [largest] + [least] * (number_of - 1), total - largest - least * (number_of - 1)
    while surplus > 0:
        movable = [i for i in range(1, number_of) if counts[i] < largest] or [i for i in range(1, number_of) if counts[i] < bound]
        mass, remaining = sum([loads[i] for i in movable]), surplus
        for i in movable:
            addition = min(bound - counts[i], max(1, remaining * loads[i] // mass), surplus)
            counts[i] = counts[i] + addition
            surplus = surplus - addition
    return np.array(counts)


def bell_draw(stream_key, dims, scale, most, shards=(), kind=jnp.bfloat16):
    level = steps_of(stream_key, dims, shards, -0.22, 0.18) if shards else 1.0
    array = jax.random.normal(stream_key, dims, jnp.float32) * scale * level
    return jnp.minimum(jnp.maximum(array, -most), most).astype(kind)


def setup_inputs(seed: int = 0) -> dict:
    key_list = jax.random.split(jax.random.key(seed), 13)
    text_embeds = draw_text_embeds(jax.random.fold_in(key_list[12], 71), 0)
    vision_tokens = bell_draw(key_list[1], (VTOK, D), 1.0, 6.0, ((0, 128), (1, 4)))
    vision_request_keys = jax.random.split(jax.random.fold_in(key_list[2], 1), VTOK // VT_GRP)
    vision_request_turns = jax.random.permutation(jax.random.fold_in(key_list[2], 3), VTOK // VT_GRP)
    vision_request = jax.vmap(lambda own, number: deal_out(jax.random.fold_in(key_list[2], 2), own, number, VT_GRP, REQUESTS, 1, CAP, 2))(vision_request_keys, vision_request_turns).reshape((VTOK, 1))
    image_start = with_ends(jax.random.randint(key_list[3], (REQUESTS,), 1, 17), jax.random.fold_in(key_list[3], 1), 1, 16).astype(jnp.int32)
    lengths = with_ends(jax.random.randint(key_list[4], (REQUESTS,), IMG_MAX + 17, SEQ_LEN + 1), jax.random.fold_in(key_list[4], 1), IMG_MAX + 17, SEQ_LEN).astype(jnp.int32)
    attn_gain = jnp.clip(1.0 + 0.1 * jax.random.normal(key_list[5], (D,), jnp.float32), 0.5, 1.5)
    w_query = draw_w_query(jax.random.fold_in(key_list[12], 71), 0)
    w_key = draw_w_key(jax.random.fold_in(key_list[12], 71), 0)
    w_value = bell_draw(key_list[8], (D, ATTN), D ** -0.5, 0.09375, ((0, 128), (1, 4)))
    w_out = bell_draw(key_list[9], (ATTN, D), ATTN ** -0.5, 0.125, ((1, 128),))
    final_gain = jnp.clip(1.0 + 0.15 * jax.random.normal(key_list[10], (D,), jnp.float32), 0.25, 1.75)
    lm_head = bell_draw(key_list[11], (D, VOCAB), (D // 9) ** -0.5, 0.25, ((1, 128),))
    return {"text_embeds": text_embeds, "vision_tokens": vision_tokens, "vision_request": vision_request, "image_start": image_start, "lengths": lengths, "attn_gain": attn_gain, "w_query": w_query, "w_key": w_key, "w_value": w_value, "w_out": w_out, "final_gain": final_gain, "lm_head": lm_head}


norm_epsilon = 1e-05

def reference(text_embeds, vision_tokens, vision_request, image_start, lengths, attn_gain, w_query, w_key, w_value, w_out, final_gain, lm_head):
    destination = vision_request[:, 0].astype(jnp.int32)
    onehot = (destination[:, None] == jnp.arange(REQUESTS, dtype=jnp.int32)[None, :]).astype(jnp.int32)
    ranking = lax.optimization_barrier(jnp.sum((jnp.cumsum(onehot, axis=0) - onehot) * onehot, axis=1)).astype(jnp.int32)
    positions = (destination * SEQ_LEN + jnp.take(image_start, destination) + ranking).astype(jnp.int32)
    states = text_embeds.at[positions].set(vision_tokens).reshape(REQUESTS, SEQ_LEN, D)

    def per_request(inputs):
        rows, length = inputs
        widened = rows.astype(jnp.float32)
        normed = (widened * lax.rsqrt(lax.optimization_barrier(jnp.mean(widened * widened, axis=1, keepdims=True)) + norm_epsilon) * attn_gain).astype(jnp.bfloat16)
        key_rows = jnp.dot(normed, w_key, preferred_element_type=jnp.float32).astype(jnp.bfloat16)
        value_rows = jnp.dot(normed, w_value, preferred_element_type=jnp.float32).astype(jnp.bfloat16)
        last_index = (length - 1).astype(jnp.int32)
        last_row = lax.dynamic_slice_in_dim(normed, last_index, 1, 0)
        query_row = jnp.dot(last_row, w_query, preferred_element_type=jnp.float32).astype(jnp.bfloat16)
        query_heads = query_row.reshape(HEADS, HD).astype(jnp.float32)
        key_heads = key_rows.reshape(SEQ_LEN, HEADS, HD).astype(jnp.float32)
        value_heads = value_rows.reshape(SEQ_LEN, HEADS, HD).astype(jnp.float32)
        scores = jnp.einsum('hc,jhc->hj', query_heads, key_heads) / math.sqrt(HD)
        live_keys = jnp.arange(SEQ_LEN, dtype=jnp.int32) < length
        scores = jnp.where(live_keys[None, :], scores, -jnp.inf)
        peak = lax.optimization_barrier(jnp.max(scores, axis=1, keepdims=True))
        shifted = jnp.exp(scores - peak)
        weights = (shifted / lax.optimization_barrier(jnp.sum(shifted, axis=1, keepdims=True))).astype(jnp.bfloat16)
        attended = jnp.einsum('hj,jhc->hc', weights.astype(jnp.float32), value_heads).astype(jnp.bfloat16)
        final_text = lax.dynamic_slice_in_dim(rows, last_index, 1, 0)[0]
        return (attended.reshape(HEADS * HD), final_text)
    attended, final_text = lax.map(per_request, (states, lengths))
    residual_out = final_text.astype(jnp.float32) + jnp.dot(attended, w_out, preferred_element_type=jnp.float32)
    mean_square = lax.optimization_barrier(jnp.mean(residual_out * residual_out, axis=1))
    scaled_out = (residual_out * final_gain).astype(jnp.bfloat16)
    logits = jnp.dot(scaled_out, lm_head, preferred_element_type=jnp.float32)
    max_logit = lax.optimization_barrier(jnp.max(logits * lax.rsqrt(mean_square + norm_epsilon)[:, None], axis=1))
    return (jnp.sqrt(mean_square), max_logit)
```

```python
import math

import jax
import jax.numpy as jnp
from jax import lax
from jax.sharding import PartitionSpec as P

HD = 128


norm_epsilon = 1e-05


def row_norm(rows, gain):
    widened = rows.astype(jnp.float32)
    return (
        widened
        * lax.rsqrt(jnp.mean(widened * widened, axis=1, keepdims=True) + norm_epsilon)
        * gain
    ).astype(jnp.bfloat16)


def pack_slots(tokens, destination, slot_index, groups, capacity):
    return (
        jnp.zeros((groups, capacity, tokens.shape[1]), jnp.bfloat16)
        .at[destination, slot_index]
        .set(tokens)
    )


def gather_by_exchange(piece, axis_name, count):
    spread = jnp.broadcast_to(piece[None], (count,) + piece.shape)
    return lax.all_to_all(spread, axis_name, split_axis=0, concat_axis=0, tiled=True)


def local(
    text_embeds,
    vision_tokens,
    vision_request,
    image_start,
    lengths,
    attn_gain,
    w_query,
    w_key,
    w_value,
    w_out,
    final_gain,
    lm_head,
):
    groups = lax.axis_size("fsdp")
    seq_count = lax.axis_size("seq")
    group_index = lax.axis_index("fsdp")
    seq_index = lax.axis_index("seq")
    seq_len = text_embeds.shape[0]
    width = text_embeds.shape[1]
    columns = w_key.shape[1]
    dpiece = width // groups
    quarter = groups // seq_count
    capacity = max(2, 2 * vision_tokens.shape[0] // groups)
    last_index = lengths[0] - 1
    final_text = lax.dynamic_slice_in_dim(text_embeds, last_index, 1, 0)
    text_pieces = final_text.reshape(groups, dpiece)
    destination = vision_request[:, 0]
    onehot = (destination[:, None] == jnp.arange(groups, dtype=jnp.int32)[None, :]).astype(
        jnp.int32
    )
    slot_index = jnp.sum((jnp.cumsum(onehot, axis=0) - onehot) * onehot, axis=1)
    counts = jnp.sum(onehot, axis=0)
    full_vision = lax.all_gather(vision_tokens, "seq", axis=1, tiled=True)
    outbox = pack_slots(full_vision, destination, slot_index, groups, capacity)
    received, arrived, text_part = (
        lax.all_to_all(outbox, "fsdp", split_axis=0, concat_axis=0, tiled=True),
        lax.all_to_all(counts[:, None], "fsdp", split_axis=0, concat_axis=0, tiled=True),
        lax.all_to_all(text_pieces, "fsdp", split_axis=0, concat_axis=0, tiled=True),
    )
    occupied = (
        (jnp.arange(capacity, dtype=jnp.int32)[None, :] < arrived).astype(jnp.int32).reshape(-1)
    )
    ranking = jnp.cumsum(occupied) - occupied
    positions = jnp.where(occupied > 0, image_start[0] + ranking, seq_len)
    states = text_embeds.at[positions].set(received.reshape(-1, width), mode="drop")
    normed = row_norm(states, attn_gain)
    last_row = lax.dynamic_slice_in_dim(normed, last_index, 1, 0)
    query_sum = jnp.dot(
        last_row,
        lax.all_gather(w_query, "fsdp", axis=0, tiled=True),
        preferred_element_type=jnp.float32,
    )
    key_sum = jnp.dot(
        normed,
        lax.all_gather(w_key, "fsdp", axis=0, tiled=True),
        preferred_element_type=jnp.float32,
    )
    value_sum = jnp.dot(
        normed,
        lax.all_gather(w_value, "fsdp", axis=0, tiled=True),
        preferred_element_type=jnp.float32,
    )
    heads_local = columns // HD
    query_heads = query_sum.astype(jnp.bfloat16).reshape(heads_local, HD)
    key_heads = key_sum.astype(jnp.bfloat16).reshape(seq_len, heads_local, HD)
    value_heads = value_sum.astype(jnp.bfloat16).reshape(seq_len, heads_local, HD)
    scores = jnp.einsum(
        "hc,jhc->hj", query_heads, key_heads, preferred_element_type=jnp.float32
    ) / math.sqrt(HD)
    live_keys = jnp.arange(seq_len, dtype=jnp.int32) < lengths[0]
    scores = jnp.where(live_keys[None, :], scores, -jnp.inf)
    peak = jnp.max(scores, axis=1, keepdims=True)
    shifted = jnp.exp(scores - peak)
    weights = (shifted / jnp.sum(shifted, axis=1, keepdims=True)).astype(jnp.bfloat16)
    attended = (
        jnp.einsum("hj,jhc->hc", weights, value_heads, preferred_element_type=jnp.float32)
        .astype(jnp.bfloat16)
        .reshape(1, columns)
    )
    attended_seq = gather_by_exchange(attended[0], "fsdp", groups)
    out_rows = lax.dynamic_slice_in_dim(w_out, seq_index * columns, columns, 0)
    partial_out = jnp.dot(attended_seq, out_rows, preferred_element_type=jnp.float32)
    out_mine = lax.psum_scatter(partial_out, "seq", scatter_dimension=0, tiled=True)
    text_mine = lax.dynamic_slice_in_dim(text_part, seq_index * quarter, quarter, 0)
    residual_out = text_mine.astype(jnp.float32) + out_mine
    residual_all = gather_by_exchange(residual_out, "fsdp", groups)
    last_state = jnp.transpose(residual_all, (1, 0, 2)).reshape(quarter, width)
    mean_square = jnp.mean(last_state * last_state, axis=1)
    scaled_out = (last_state * final_gain[None, :]).astype(jnp.bfloat16)
    logits = jnp.dot(scaled_out, lm_head, preferred_element_type=jnp.float32)
    local_max = jnp.max(logits, axis=1) * lax.rsqrt(mean_square + norm_epsilon)
    max_all = gather_by_exchange(local_max, "fsdp", groups)
    max_logit = jnp.max(max_all, axis=0)
    return (jnp.sqrt(mean_square), max_logit)


def solution(mesh):
    return jax.shard_map(
        local,
        mesh=mesh,
        in_specs=(
            P("fsdp", None),
            P("fsdp", "seq"),
            P("fsdp", None),
            P("fsdp"),
            P("fsdp"),
            P(),
            P("fsdp", "seq"),
            P("fsdp", "seq"),
            P("fsdp", "seq"),
            P(None, "fsdp"),
            P(),
            P(None, "fsdp"),
        ),
        out_specs=(P("seq"), P("seq")),
        check_vma=False,
    )
```

```python
import math

import jax
import jax.numpy as jnp
from jax import lax
from jax.sharding import PartitionSpec as P

HD = 128


norm_epsilon = 1e-05


def row_norm(rows, gain):
    widened = rows.astype(jnp.float32)
    return (
        widened
        * lax.rsqrt(jnp.mean(widened * widened, axis=1, keepdims=True) + norm_epsilon)
        * gain
    ).astype(jnp.bfloat16)


def exchange(rows, axis_name):
    return lax.all_to_all(rows, axis_name, split_axis=0, concat_axis=0, tiled=True)


def gather_by_exchange(piece, axis_name, count):
    spread = jnp.broadcast_to(piece[None], (count,) + piece.shape)
    return exchange(spread, axis_name)


def select_rows(selector, rows):
    return jnp.dot(
        selector.astype(jnp.bfloat16), rows, preferred_element_type=jnp.float32
    ).astype(jnp.bfloat16)


def local(
    text_embeds,
    vision_tokens,
    vision_request,
    image_start,
    lengths,
    attn_gain,
    w_query,
    w_key,
    w_value,
    w_out,
    final_gain,
    lm_head,
):
    groups = lax.axis_size("fsdp")
    seq_count = lax.axis_size("seq")
    seq_index = lax.axis_index("seq")
    seq_len = text_embeds.shape[0]
    width = text_embeds.shape[1]
    columns = w_key.shape[1]
    heads_local = columns // HD
    dpiece = width // groups
    quarter = groups // seq_count
    capacity = max(2, 2 * vision_tokens.shape[0] // groups)
    last_index = lengths[0] - 1

    final_text = lax.dynamic_slice_in_dim(text_embeds, last_index, 1, 0)
    last_normed = row_norm(final_text, attn_gain)
    pieces = jnp.stack(
        [final_text.reshape(groups, dpiece), last_normed.reshape(groups, dpiece)], axis=1
    )
    pieces_in = exchange(pieces, "fsdp")
    text_part = pieces_in[:, 0]
    normed_part = pieces_in[:, 1]

    query_partial = jnp.dot(normed_part, w_query, preferred_element_type=jnp.float32)
    query_mine = jnp.sum(exchange(query_partial, "fsdp"), axis=0).astype(jnp.bfloat16)
    query_all = gather_by_exchange(query_mine, "fsdp", groups)

    query_heads = query_all.astype(jnp.float32).reshape(groups, heads_local, HD)
    key_rows = w_key.astype(jnp.float32).reshape(dpiece, heads_local, HD)
    probe_part = jnp.einsum(
        "rhc,dhc->rhd", query_heads, key_rows, precision=lax.Precision.HIGHEST
    )
    probe_in = exchange(probe_part, "fsdp")
    probe = jnp.transpose(probe_in, (1, 0, 2)).reshape(heads_local, width)

    destination = vision_request[:, 0]
    onehot = (destination[:, None] == jnp.arange(groups, dtype=jnp.int32)[None, :]).astype(
        jnp.int32
    )
    slot_index = jnp.sum((jnp.cumsum(onehot, axis=0) - onehot) * onehot, axis=1)
    counts = jnp.sum(onehot, axis=0)
    full_vision = lax.all_gather(vision_tokens, "seq", axis=1, tiled=True)
    slot_of = destination * capacity + slot_index
    outbox_select = (
        jnp.arange(groups * capacity, dtype=jnp.int32)[:, None] == slot_of[None, :]
    )
    outbox = select_rows(outbox_select, full_vision).reshape(groups, capacity, width)
    received = exchange(outbox, "fsdp")
    arrived = exchange(counts[:, None], "fsdp")
    occupied = (
        (jnp.arange(capacity, dtype=jnp.int32)[None, :] < arrived).astype(jnp.int32).reshape(-1)
    )
    ranking = jnp.cumsum(occupied) - occupied
    positions = jnp.where(occupied > 0, image_start[0] + ranking, seq_len)
    place = jnp.arange(seq_len, dtype=jnp.int32)[:, None] == positions[None, :]
    placed = select_rows(place, received.reshape(-1, width))
    replaced = jnp.any(place, axis=1, keepdims=True)
    states = jnp.where(replaced, placed, text_embeds)
    normed = row_norm(states, attn_gain)

    value_sum = jnp.dot(
        normed,
        lax.all_gather(w_value, "fsdp", axis=0, tiled=True),
        preferred_element_type=jnp.float32,
    )
    value_heads = value_sum.astype(jnp.bfloat16).reshape(seq_len, heads_local, HD)
    scores = jnp.dot(
        normed.astype(jnp.float32), probe.T, precision=lax.Precision.HIGHEST
    ).T / math.sqrt(HD)
    live_keys = jnp.arange(seq_len, dtype=jnp.int32) < lengths[0]
    scores = jnp.where(live_keys[None, :], scores, -jnp.inf)
    peak = jnp.max(scores, axis=1, keepdims=True)
    shifted = jnp.exp(scores - peak)
    weights = (shifted / jnp.sum(shifted, axis=1, keepdims=True)).astype(jnp.bfloat16)
    attended = (
        jnp.einsum("hj,jhc->hc", weights, value_heads, preferred_element_type=jnp.float32)
        .astype(jnp.bfloat16)
        .reshape(columns)
    )

    attended_seq = gather_by_exchange(attended, "fsdp", groups)
    out_rows = lax.dynamic_slice_in_dim(w_out, seq_index * columns, columns, 0)
    partial_out = jnp.dot(attended_seq, out_rows, preferred_element_type=jnp.float32)
    out_mine = lax.psum_scatter(partial_out, "seq", scatter_dimension=0, tiled=True)
    text_mine = lax.dynamic_slice_in_dim(text_part, seq_index * quarter, quarter, 0)
    residual_out = text_mine.astype(jnp.float32) + out_mine
    residual_all = gather_by_exchange(residual_out, "fsdp", groups)
    last_state = jnp.transpose(residual_all, (1, 0, 2)).reshape(quarter, width)
    mean_square = jnp.mean(last_state * last_state, axis=1)
    scaled_out = (last_state * final_gain[None, :]).astype(jnp.bfloat16)
    logits = jnp.dot(scaled_out, lm_head, preferred_element_type=jnp.float32)
    local_max = jnp.max(logits, axis=1) * lax.rsqrt(mean_square + norm_epsilon)
    max_all = gather_by_exchange(local_max, "fsdp", groups)
    max_logit = jnp.max(max_all, axis=0)
    return (jnp.sqrt(mean_square), max_logit)


def solution(mesh):
    return jax.shard_map(
        local,
        mesh=mesh,
        in_specs=(
            P("fsdp", None),
            P("fsdp", "seq"),
            P("fsdp", None),
            P("fsdp"),
            P("fsdp"),
            P(),
            P("fsdp", "seq"),
            P("fsdp", "seq"),
            P("fsdp", "seq"),
            P(None, "fsdp"),
            P(),
            P(None, "fsdp"),
        ),
        out_specs=(P("seq"), P("seq")),
        check_vma=False,
    )
```

```python
import math

import jax
import jax.numpy as jnp
from jax import lax
from jax.sharding import PartitionSpec as P

HD = 128


norm_epsilon = 1e-05


def row_norm(rows, gain):
    widened = rows.astype(jnp.float32)
    return (
        widened
        * lax.rsqrt(jnp.mean(widened * widened, axis=1, keepdims=True) + norm_epsilon)
        * gain
    ).astype(jnp.bfloat16)


def exchange(rows, axis_name):
    return lax.all_to_all(rows, axis_name, split_axis=0, concat_axis=0, tiled=True)


def gather_by_exchange(piece, axis_name, count):
    spread = jnp.broadcast_to(piece[None], (count,) + piece.shape)
    return exchange(spread, axis_name)


def select_rows(selector, rows):
    return jnp.dot(
        selector.astype(jnp.bfloat16), rows, preferred_element_type=jnp.float32
    ).astype(jnp.bfloat16)


def local(
    text_embeds,
    vision_tokens,
    vision_request,
    image_start,
    lengths,
    attn_gain,
    w_query,
    w_key,
    w_value,
    w_out,
    final_gain,
    lm_head,
):
    groups = lax.axis_size("fsdp")
    seq_count = lax.axis_size("seq")
    seq_index = lax.axis_index("seq")
    seq_len = text_embeds.shape[0]
    width = text_embeds.shape[1]
    columns = w_key.shape[1]
    heads_local = columns // HD
    dpiece = width // groups
    quarter = groups // seq_count
    capacity = max(2, 2 * vision_tokens.shape[0] // groups)
    last_index = lengths[0] - 1

    destination = vision_request[:, 0]
    onehot = (destination[:, None] == jnp.arange(groups, dtype=jnp.int32)[None, :]).astype(
        jnp.int32
    )
    slot_index = jnp.sum((jnp.cumsum(onehot, axis=0) - onehot) * onehot, axis=1)
    counts = jnp.sum(onehot, axis=0)

    final_text = lax.dynamic_slice_in_dim(text_embeds, last_index, 1, 0)
    last_normed = row_norm(final_text, attn_gain)
    pieces = jnp.stack(
        [
            final_text.reshape(groups, dpiece),
            last_normed.reshape(groups, dpiece),
            jnp.broadcast_to(counts.astype(jnp.bfloat16)[:, None], (groups, dpiece)),
        ],
        axis=1,
    )
    pieces_in = exchange(pieces, "fsdp")
    text_part = pieces_in[:, 0]
    normed_part = pieces_in[:, 1]
    arrived = pieces_in[:, 2, :1].astype(jnp.int32)

    query_partial = jnp.dot(normed_part, w_query, preferred_element_type=jnp.float32)
    query_all = lax.psum(query_partial, "fsdp").astype(jnp.bfloat16)

    query_heads = query_all.astype(jnp.float32).reshape(groups, heads_local, HD)
    key_rows = w_key.astype(jnp.float32).reshape(dpiece, heads_local, HD)
    probe_part = jnp.einsum(
        "rhc,dhc->rhd", query_heads, key_rows, precision=lax.Precision.HIGHEST
    )
    probe_in = exchange(probe_part, "fsdp")
    probe = jnp.transpose(probe_in, (1, 0, 2)).reshape(heads_local, width)

    full_vision = lax.all_gather(vision_tokens, "seq", axis=1, tiled=True)
    slot_of = destination * capacity + slot_index
    outbox_select = (
        jnp.arange(groups * capacity, dtype=jnp.int32)[:, None] == slot_of[None, :]
    )
    outbox = select_rows(outbox_select, full_vision).reshape(groups, capacity, width)
    received = exchange(outbox, "fsdp")
    occupied = (
        (jnp.arange(capacity, dtype=jnp.int32)[None, :] < arrived).astype(jnp.int32).reshape(-1)
    )
    ranking = jnp.cumsum(occupied) - occupied
    positions = jnp.where(occupied > 0, image_start[0] + ranking, seq_len)
    place = jnp.arange(seq_len, dtype=jnp.int32)[:, None] == positions[None, :]
    placed = select_rows(place, received.reshape(-1, width))
    replaced = jnp.any(place, axis=1, keepdims=True)
    states = jnp.where(replaced, placed, text_embeds)
    normed = row_norm(states, attn_gain)

    scores = jnp.dot(
        normed.astype(jnp.float32), probe.T, precision=lax.Precision.HIGHEST
    ).T / math.sqrt(HD)
    live_keys = jnp.arange(seq_len, dtype=jnp.int32) < lengths[0]
    scores = jnp.where(live_keys[None, :], scores, -jnp.inf)
    peak = jnp.max(scores, axis=1, keepdims=True)
    shifted = jnp.exp(scores - peak)
    weights = (shifted / jnp.sum(shifted, axis=1, keepdims=True)).astype(jnp.bfloat16)

    mixed = jnp.dot(weights, normed, preferred_element_type=jnp.float32)
    mixed_pieces = jnp.transpose(mixed.reshape(heads_local, groups, dpiece), (1, 0, 2))
    mixed_in = exchange(mixed_pieces, "fsdp")
    value_rows = w_value.astype(jnp.float32).reshape(dpiece, heads_local, HD)
    attended_partial = jnp.einsum(
        "rhd,dhc->rhc", mixed_in, value_rows, precision=lax.Precision.HIGHEST
    ).reshape(groups, columns)
    attended_seq = lax.psum(attended_partial, "fsdp").astype(jnp.bfloat16)
    out_rows = lax.dynamic_slice_in_dim(w_out, seq_index * columns, columns, 0)
    partial_out = jnp.dot(attended_seq, out_rows, preferred_element_type=jnp.float32)
    out_mine = lax.psum_scatter(partial_out, "seq", scatter_dimension=0, tiled=True)
    text_mine = lax.dynamic_slice_in_dim(text_part, seq_index * quarter, quarter, 0)
    residual_out = text_mine.astype(jnp.float32) + out_mine
    residual_all = gather_by_exchange(residual_out, "fsdp", groups)
    last_state = jnp.transpose(residual_all, (1, 0, 2)).reshape(quarter, width)
    mean_square = jnp.mean(last_state * last_state, axis=1)
    scaled_out = (last_state * final_gain[None, :]).astype(jnp.bfloat16)
    logits = jnp.dot(scaled_out, lm_head, preferred_element_type=jnp.float32)
    local_max = jnp.max(logits, axis=1) * lax.rsqrt(mean_square + norm_epsilon)
    max_all = gather_by_exchange(local_max, "fsdp", groups)
    max_logit = jnp.max(max_all, axis=0)
    return (jnp.sqrt(mean_square), max_logit)


def solution(mesh):
    return jax.shard_map(
        local,
        mesh=mesh,
        in_specs=(
            P("fsdp", None),
            P("fsdp", "seq"),
            P("fsdp", None),
            P("fsdp"),
            P("fsdp"),
            P(),
            P("fsdp", "seq"),
            P("fsdp", "seq"),
            P("fsdp", "seq"),
            P(None, "fsdp"),
            P(),
            P(None, "fsdp"),
        ),
        out_specs=(P("seq"), P("seq")),
        check_vma=False,
    )
```

```python
import math

import jax
import jax.numpy as jnp
from jax import lax
from jax.sharding import PartitionSpec as P

HD = 128


norm_epsilon = 1e-05


def row_norm(rows, gain):
    widened = rows.astype(jnp.float32)
    return (
        widened
        * lax.rsqrt(jnp.mean(widened * widened, axis=1, keepdims=True) + norm_epsilon)
        * gain
    ).astype(jnp.bfloat16)


def exchange(rows, axis_name):
    return lax.all_to_all(rows, axis_name, split_axis=0, concat_axis=0, tiled=True)


def gather_by_exchange(piece, axis_name, count):
    spread = jnp.broadcast_to(piece[None], (count,) + piece.shape)
    return exchange(spread, axis_name)


def select_rows(selector, rows):
    return jnp.dot(
        selector.astype(jnp.bfloat16), rows, preferred_element_type=jnp.float32
    ).astype(jnp.bfloat16)


def local(
    text_embeds,
    vision_tokens,
    vision_request,
    image_start,
    lengths,
    attn_gain,
    w_query,
    w_key,
    w_value,
    w_out,
    final_gain,
    lm_head,
):
    groups = lax.axis_size("fsdp")
    seq_count = lax.axis_size("seq")
    seq_index = lax.axis_index("seq")
    seq_len = text_embeds.shape[0]
    width = text_embeds.shape[1]
    columns = w_key.shape[1]
    heads_local = columns // HD
    dpiece = width // groups
    quarter = groups // seq_count
    capacity = max(2, 2 * vision_tokens.shape[0] // groups)
    last_index = lengths[0] - 1

    destination = vision_request[:, 0]
    onehot = (destination[:, None] == jnp.arange(groups, dtype=jnp.int32)[None, :]).astype(
        jnp.int32
    )
    slot_index = jnp.sum((jnp.cumsum(onehot, axis=0) - onehot) * onehot, axis=1)
    counts = jnp.sum(onehot, axis=0)

    final_text = lax.dynamic_slice_in_dim(text_embeds, last_index, 1, 0)
    last_normed = row_norm(final_text, attn_gain)
    pieces = jnp.stack(
        [
            final_text.reshape(groups, dpiece),
            last_normed.reshape(groups, dpiece),
            jnp.broadcast_to(counts.astype(jnp.bfloat16)[:, None], (groups, dpiece)),
        ],
        axis=1,
    )
    pieces_in = exchange(pieces, "fsdp")
    text_part = pieces_in[:, 0]
    normed_part = pieces_in[:, 1]
    arrived = pieces_in[:, 2, :1].astype(jnp.int32)

    query_partial = jnp.dot(normed_part, w_query, preferred_element_type=jnp.float32)
    query_mine = jnp.sum(exchange(query_partial, "fsdp"), axis=0).astype(jnp.bfloat16)
    query_all = gather_by_exchange(query_mine, "fsdp", groups)

    query_heads = query_all.astype(jnp.float32).reshape(groups, heads_local, HD)
    key_rows = w_key.astype(jnp.float32).reshape(dpiece, heads_local, HD)
    probe_part = jnp.einsum(
        "rhc,dhc->rhd", query_heads, key_rows, precision=lax.Precision.HIGHEST
    )
    probe_in = exchange(probe_part, "fsdp")
    probe = jnp.transpose(probe_in, (1, 0, 2)).reshape(heads_local, width)

    full_vision = lax.all_gather(vision_tokens, "seq", axis=1, tiled=True)
    slot_of = destination * capacity + slot_index
    outbox_select = (
        jnp.arange(groups * capacity, dtype=jnp.int32)[:, None] == slot_of[None, :]
    )
    outbox = select_rows(outbox_select, full_vision).reshape(groups, capacity, width)
    received = exchange(outbox, "fsdp")
    occupied = (
        (jnp.arange(capacity, dtype=jnp.int32)[None, :] < arrived).astype(jnp.int32).reshape(-1)
    )
    ranking = jnp.cumsum(occupied) - occupied
    positions = jnp.where(occupied > 0, image_start[0] + ranking, seq_len)
    place = jnp.arange(seq_len, dtype=jnp.int32)[:, None] == positions[None, :]
    placed = select_rows(place, received.reshape(-1, width))
    replaced = jnp.any(place, axis=1, keepdims=True)
    states = jnp.where(replaced, placed, text_embeds)
    normed = row_norm(states, attn_gain)

    value_sum = jnp.dot(
        normed,
        lax.all_gather(w_value, "fsdp", axis=0, tiled=True),
        preferred_element_type=jnp.float32,
    )
    value_heads = value_sum.astype(jnp.bfloat16).reshape(seq_len, heads_local, HD)
    scores = jnp.dot(
        normed.astype(jnp.float32), probe.T, precision=lax.Precision.HIGHEST
    ).T / math.sqrt(HD)
    live_keys = jnp.arange(seq_len, dtype=jnp.int32) < lengths[0]
    scores = jnp.where(live_keys[None, :], scores, -jnp.inf)
    peak = jnp.max(scores, axis=1, keepdims=True)
    shifted = jnp.exp(scores - peak)
    weights = (shifted / jnp.sum(shifted, axis=1, keepdims=True)).astype(jnp.bfloat16)
    attended = (
        jnp.einsum("hj,jhc->hc", weights, value_heads, preferred_element_type=jnp.float32)
        .astype(jnp.bfloat16)
        .reshape(columns)
    )

    attended_seq = gather_by_exchange(attended, "fsdp", groups)
    out_rows = lax.dynamic_slice_in_dim(w_out, seq_index * columns, columns, 0)
    partial_out = jnp.dot(attended_seq, out_rows, preferred_element_type=jnp.float32)
    out_mine = lax.psum_scatter(partial_out, "seq", scatter_dimension=0, tiled=True)
    text_mine = lax.dynamic_slice_in_dim(text_part, seq_index * quarter, quarter, 0)
    residual_out = text_mine.astype(jnp.float32) + out_mine
    gain_part = lax.dynamic_slice_in_dim(final_gain, lax.axis_index("fsdp") * dpiece, dpiece, 0)
    scaled_part = (residual_out * gain_part[None, :]).astype(jnp.bfloat16)
    square_part = jnp.sum(residual_out * residual_out, axis=1, keepdims=True)
    square_high = square_part.astype(jnp.bfloat16)
    square_low = (square_part - square_high.astype(jnp.float32)).astype(jnp.bfloat16)
    payload = jnp.concatenate([scaled_part, square_high, square_low], axis=1)
    payload_all = gather_by_exchange(payload, "fsdp", groups)
    scaled_out = jnp.transpose(payload_all[:, :, :dpiece], (1, 0, 2)).reshape(quarter, width)
    square_sum = jnp.sum(
        payload_all[:, :, dpiece:].astype(jnp.float32), axis=(0, 2)
    )
    mean_square = square_sum / width
    logits = jnp.dot(scaled_out, lm_head, preferred_element_type=jnp.float32)
    local_max = jnp.max(logits, axis=1) * lax.rsqrt(mean_square + norm_epsilon)
    max_all = gather_by_exchange(local_max, "fsdp", groups)
    max_logit = jnp.max(max_all, axis=0)
    return (jnp.sqrt(mean_square), max_logit)


def solution(mesh):
    return jax.shard_map(
        local,
        mesh=mesh,
        in_specs=(
            P("fsdp", None),
            P("fsdp", "seq"),
            P("fsdp", None),
            P("fsdp"),
            P("fsdp"),
            P(),
            P("fsdp", "seq"),
            P("fsdp", "seq"),
            P("fsdp", "seq"),
            P(None, "fsdp"),
            P(),
            P(None, "fsdp"),
        ),
        out_specs=(P("seq"), P("seq")),
        check_vma=False,
    )
```

```python
import math

import jax
import jax.numpy as jnp
from jax import lax
from jax.sharding import PartitionSpec as P

HD = 128


norm_epsilon = 1e-05


def row_norm(rows, gain):
    widened = rows.astype(jnp.float32)
    return (
        widened
        * lax.rsqrt(jnp.mean(widened * widened, axis=1, keepdims=True) + norm_epsilon)
        * gain
    ).astype(jnp.bfloat16)


def exchange(rows, axis_name):
    return lax.all_to_all(rows, axis_name, split_axis=0, concat_axis=0, tiled=True)


def gather_by_exchange(piece, axis_name, count):
    spread = jnp.broadcast_to(piece[None], (count,) + piece.shape)
    return exchange(spread, axis_name)


def select_rows(selector, rows):
    return jnp.dot(
        selector.astype(jnp.bfloat16), rows, preferred_element_type=jnp.float32
    ).astype(jnp.bfloat16)


def local(
    text_embeds,
    vision_tokens,
    vision_request,
    image_start,
    lengths,
    attn_gain,
    w_query,
    w_key,
    w_value,
    w_out,
    final_gain,
    lm_head,
):
    groups = lax.axis_size("fsdp")
    seq_count = lax.axis_size("seq")
    seq_index = lax.axis_index("seq")
    seq_len = text_embeds.shape[0]
    width = text_embeds.shape[1]
    columns = w_key.shape[1]
    heads_local = columns // HD
    dpiece = width // groups
    quarter = groups // seq_count
    capacity = max(2, 2 * vision_tokens.shape[0] // groups)
    last_index = lengths[0] - 1

    destination = vision_request[:, 0]
    onehot = (destination[:, None] == jnp.arange(groups, dtype=jnp.int32)[None, :]).astype(
        jnp.int32
    )
    slot_index = jnp.sum((jnp.cumsum(onehot, axis=0) - onehot) * onehot, axis=1)
    counts = jnp.sum(onehot, axis=0)

    final_text = lax.dynamic_slice_in_dim(text_embeds, last_index, 1, 0)
    last_normed = row_norm(final_text, attn_gain)
    pieces = jnp.stack(
        [
            final_text.reshape(groups, dpiece),
            last_normed.reshape(groups, dpiece),
            jnp.broadcast_to(counts.astype(jnp.bfloat16)[:, None], (groups, dpiece)),
        ],
        axis=1,
    )
    pieces_in = exchange(pieces, "fsdp")
    text_part = pieces_in[:, 0]
    normed_part = pieces_in[:, 1]
    arrived = pieces_in[:, 2, :1].astype(jnp.int32)

    query_partial = jnp.dot(normed_part, w_query, preferred_element_type=jnp.float32)
    query_mine = jnp.sum(exchange(query_partial, "fsdp"), axis=0).astype(jnp.bfloat16)
    query_padded = jnp.zeros((1, width), jnp.bfloat16).at[0, :columns].set(query_mine)
    query_all = lax.all_gather(query_padded, "fsdp", axis=0, tiled=True)[:, :columns]

    query_heads = query_all.astype(jnp.float32).reshape(groups, heads_local, HD)
    key_rows = w_key.astype(jnp.float32).reshape(dpiece, heads_local, HD)
    probe_part = jnp.einsum(
        "rhc,dhc->rhd", query_heads, key_rows, precision=lax.Precision.HIGHEST
    )
    probe_in = exchange(probe_part, "fsdp")
    probe = jnp.transpose(probe_in, (1, 0, 2)).reshape(heads_local, width)

    full_vision = lax.all_gather(vision_tokens, "seq", axis=1, tiled=True)
    slot_of = destination * capacity + slot_index
    outbox_select = (
        jnp.arange(groups * capacity, dtype=jnp.int32)[:, None] == slot_of[None, :]
    )
    outbox = select_rows(outbox_select, full_vision).reshape(groups, capacity, width)
    received = exchange(outbox, "fsdp")
    occupied = (
        (jnp.arange(capacity, dtype=jnp.int32)[None, :] < arrived).astype(jnp.int32).reshape(-1)
    )
    ranking = jnp.cumsum(occupied) - occupied
    positions = jnp.where(occupied > 0, image_start[0] + ranking, seq_len)
    place = jnp.arange(seq_len, dtype=jnp.int32)[:, None] == positions[None, :]
    placed = select_rows(place, received.reshape(-1, width))
    replaced = jnp.any(place, axis=1, keepdims=True)
    states = jnp.where(replaced, placed, text_embeds)
    normed = row_norm(states, attn_gain)

    value_sum = jnp.dot(
        normed,
        lax.all_gather(w_value, "fsdp", axis=0, tiled=True),
        preferred_element_type=jnp.float32,
    )
    value_heads = value_sum.astype(jnp.bfloat16).reshape(seq_len, heads_local, HD)
    scores = jnp.dot(
        normed.astype(jnp.float32), probe.T, precision=lax.Precision.HIGHEST
    ).T / math.sqrt(HD)
    live_keys = jnp.arange(seq_len, dtype=jnp.int32) < lengths[0]
    scores = jnp.where(live_keys[None, :], scores, -jnp.inf)
    peak = jnp.max(scores, axis=1, keepdims=True)
    shifted = jnp.exp(scores - peak)
    weights = (shifted / jnp.sum(shifted, axis=1, keepdims=True)).astype(jnp.bfloat16)
    attended = (
        jnp.einsum("hj,jhc->hc", weights, value_heads, preferred_element_type=jnp.float32)
        .astype(jnp.bfloat16)
        .reshape(columns)
    )

    attended_every = gather_by_exchange(attended, ("fsdp", "seq"), groups * seq_count)
    attended_mine = lax.dynamic_slice_in_dim(
        attended_every.reshape(groups, seq_count * columns), seq_index * quarter, quarter, 0
    )
    out_mine = jnp.dot(attended_mine, w_out, preferred_element_type=jnp.float32)
    text_mine = lax.dynamic_slice_in_dim(text_part, seq_index * quarter, quarter, 0)
    residual_out = text_mine.astype(jnp.float32) + out_mine
    gain_part = lax.dynamic_slice_in_dim(final_gain, lax.axis_index("fsdp") * dpiece, dpiece, 0)
    scaled_part = (residual_out * gain_part[None, :]).astype(jnp.bfloat16)
    square_part = jnp.sum(residual_out * residual_out, axis=1, keepdims=True)
    square_high = square_part.astype(jnp.bfloat16)
    square_low = (square_part - square_high.astype(jnp.float32)).astype(jnp.bfloat16)
    payload = jnp.concatenate([scaled_part, square_high, square_low], axis=1)
    payload_all = gather_by_exchange(payload, "fsdp", groups)
    scaled_out = jnp.transpose(payload_all[:, :, :dpiece], (1, 0, 2)).reshape(quarter, width)
    square_sum = jnp.sum(
        payload_all[:, :, dpiece:].astype(jnp.float32), axis=(0, 2)
    )
    mean_square = square_sum / width
    logits = jnp.dot(scaled_out, lm_head, preferred_element_type=jnp.float32)
    local_max = jnp.max(logits, axis=1) * lax.rsqrt(mean_square + norm_epsilon)
    max_all = gather_by_exchange(local_max, "fsdp", groups)
    max_logit = jnp.max(max_all, axis=0)
    return (jnp.sqrt(mean_square), max_logit)


def solution(mesh):
    return jax.shard_map(
        local,
        mesh=mesh,
        in_specs=(
            P("fsdp", None),
            P("fsdp", "seq"),
            P("fsdp", None),
            P("fsdp"),
            P("fsdp"),
            P(),
            P("fsdp", "seq"),
            P("fsdp", "seq"),
            P("fsdp", "seq"),
            P(None, "fsdp"),
            P(),
            P(None, "fsdp"),
        ),
        out_specs=(P("seq"), P("seq")),
        check_vma=False,
    )
```

```python
import math

import jax
import jax.numpy as jnp
from jax import lax
from jax.sharding import PartitionSpec as P

HD = 128


norm_epsilon = 1e-05


def row_norm(rows, gain):
    widened = rows.astype(jnp.float32)
    return (
        widened
        * lax.rsqrt(jnp.mean(widened * widened, axis=1, keepdims=True) + norm_epsilon)
        * gain
    ).astype(jnp.bfloat16)


def exchange(rows, axis_name):
    return lax.all_to_all(rows, axis_name, split_axis=0, concat_axis=0, tiled=True)


def gather_by_exchange(piece, axis_name, count):
    spread = jnp.broadcast_to(piece[None], (count,) + piece.shape)
    return exchange(spread, axis_name)


def select_rows(selector, rows):
    return jnp.dot(
        selector.astype(jnp.bfloat16), rows, preferred_element_type=jnp.float32
    ).astype(jnp.bfloat16)


def local(
    text_embeds,
    vision_tokens,
    vision_request,
    image_start,
    lengths,
    attn_gain,
    w_query,
    w_key,
    w_value,
    w_out,
    final_gain,
    lm_head,
):
    groups = lax.axis_size("fsdp")
    seq_count = lax.axis_size("seq")
    seq_index = lax.axis_index("seq")
    seq_len = text_embeds.shape[0]
    width = text_embeds.shape[1]
    columns = w_key.shape[1]
    heads_local = columns // HD
    dpiece = width // groups
    quarter = groups // seq_count
    capacity = max(2, 2 * vision_tokens.shape[0] // groups)
    last_index = lengths[0] - 1

    destination = vision_request[:, 0]
    onehot = (destination[:, None] == jnp.arange(groups, dtype=jnp.int32)[None, :]).astype(
        jnp.int32
    )
    slot_index = jnp.sum((jnp.cumsum(onehot, axis=0) - onehot) * onehot, axis=1)
    counts = jnp.sum(onehot, axis=0)

    final_text = lax.dynamic_slice_in_dim(text_embeds, last_index, 1, 0)
    last_normed = row_norm(final_text, attn_gain)
    pieces = jnp.stack(
        [
            final_text.reshape(groups, dpiece),
            last_normed.reshape(groups, dpiece),
            jnp.broadcast_to(counts.astype(jnp.bfloat16)[:, None], (groups, dpiece)),
        ],
        axis=1,
    )
    pieces_in = exchange(pieces, "fsdp")
    text_part = pieces_in[:, 0]
    normed_part = pieces_in[:, 1]
    arrived = pieces_in[:, 2, :1].astype(jnp.int32)

    query_partial = jnp.dot(normed_part, w_query, preferred_element_type=jnp.float32)
    query_mine = jnp.sum(exchange(query_partial, "fsdp"), axis=0).astype(jnp.bfloat16)
    query_all = gather_by_exchange(query_mine, "fsdp", groups)

    query_heads = query_all.astype(jnp.float32).reshape(groups, heads_local, HD)
    key_rows = w_key.astype(jnp.float32).reshape(dpiece, heads_local, HD)
    probe_part = jnp.einsum(
        "rhc,dhc->rhd", query_heads, key_rows, precision=lax.Precision.HIGHEST
    )
    probe_in = exchange(probe_part, "fsdp")
    probe = jnp.transpose(probe_in, (1, 0, 2)).reshape(heads_local, width)

    full_vision = lax.all_gather(vision_tokens, "seq", axis=1, tiled=True)
    dest_select = destination[None, :] == jnp.arange(groups, dtype=jnp.int32)[:, None]
    outbox = jnp.concatenate(
        [
            select_rows(dest_select & (slot_index[None, :] == slot), full_vision)
            for slot in range(capacity)
        ],
        axis=1,
    )
    received = exchange(outbox, "fsdp")
    occupied = (jnp.arange(capacity, dtype=jnp.int32)[None, :] < arrived).astype(jnp.int32)
    ranking = (jnp.cumsum(occupied.reshape(-1)) - occupied.reshape(-1)).reshape(groups, capacity)
    positions = jnp.where(occupied > 0, image_start[0] + ranking, seq_len)
    row_ids = jnp.arange(seq_len, dtype=jnp.int32)[:, None]
    placed = jnp.zeros((seq_len, width), jnp.float32)
    replaced = jnp.zeros((seq_len, 1), jnp.bool_)
    for slot in range(capacity):
        place = row_ids == positions[None, :, slot]
        placed = placed + jnp.dot(
            place.astype(jnp.bfloat16),
            received[:, slot * width : (slot + 1) * width],
            preferred_element_type=jnp.float32,
        )
        replaced = replaced | jnp.any(place, axis=1, keepdims=True)
    states = jnp.where(replaced, placed.astype(jnp.bfloat16), text_embeds)
    normed = row_norm(states, attn_gain)

    value_sum = jnp.dot(
        normed,
        lax.all_gather(w_value, "fsdp", axis=0, tiled=True),
        preferred_element_type=jnp.float32,
    )
    value_heads = value_sum.astype(jnp.bfloat16).reshape(seq_len, heads_local, HD)
    scores = jnp.dot(
        normed.astype(jnp.float32), probe.T, precision=lax.Precision.HIGHEST
    ).T / math.sqrt(HD)
    live_keys = jnp.arange(seq_len, dtype=jnp.int32) < lengths[0]
    scores = jnp.where(live_keys[None, :], scores, -jnp.inf)
    peak = jnp.max(scores, axis=1, keepdims=True)
    shifted = jnp.exp(scores - peak)
    weights = (shifted / jnp.sum(shifted, axis=1, keepdims=True)).astype(jnp.bfloat16)
    attended = (
        jnp.einsum("hj,jhc->hc", weights, value_heads, preferred_element_type=jnp.float32)
        .astype(jnp.bfloat16)
        .reshape(columns)
    )

    attended_every = gather_by_exchange(attended, ("fsdp", "seq"), groups * seq_count)
    attended_mine = lax.dynamic_slice_in_dim(
        attended_every.reshape(groups, seq_count * columns), seq_index * quarter, quarter, 0
    )
    out_mine = jnp.dot(attended_mine, w_out, preferred_element_type=jnp.float32)
    text_mine = lax.dynamic_slice_in_dim(text_part, seq_index * quarter, quarter, 0)
    residual_out = text_mine.astype(jnp.float32) + out_mine
    gain_part = lax.dynamic_slice_in_dim(final_gain, lax.axis_index("fsdp") * dpiece, dpiece, 0)
    scaled_part = (residual_out * gain_part[None, :]).astype(jnp.bfloat16)
    square_part = jnp.sum(residual_out * residual_out, axis=1, keepdims=True)
    square_high = square_part.astype(jnp.bfloat16)
    square_low = (square_part - square_high.astype(jnp.float32)).astype(jnp.bfloat16)
    payload = jnp.concatenate([scaled_part, square_high, square_low], axis=1)
    payload_all = gather_by_exchange(payload, "fsdp", groups)
    scaled_out = jnp.transpose(payload_all[:, :, :dpiece], (1, 0, 2)).reshape(quarter, width)
    square_sum = jnp.sum(
        payload_all[:, :, dpiece:].astype(jnp.float32), axis=(0, 2)
    )
    mean_square = square_sum / width
    logits = jnp.dot(scaled_out, lm_head, preferred_element_type=jnp.float32)
    local_max = jnp.max(logits, axis=1) * lax.rsqrt(mean_square + norm_epsilon)
    max_all = gather_by_exchange(local_max, "fsdp", groups)
    max_logit = jnp.max(max_all, axis=0)
    return (jnp.sqrt(mean_square), max_logit)


def solution(mesh):
    return jax.shard_map(
        local,
        mesh=mesh,
        in_specs=(
            P("fsdp", None),
            P("fsdp", "seq"),
            P("fsdp", None),
            P("fsdp"),
            P("fsdp"),
            P(),
            P("fsdp", "seq"),
            P("fsdp", "seq"),
            P("fsdp", "seq"),
            P(None, "fsdp"),
            P(),
            P(None, "fsdp"),
        ),
        out_specs=(P("seq"), P("seq")),
        check_vma=False,
    )
```

```python
import math

import functools

import jax
import jax.numpy as jnp
from jax import lax
from jax.experimental import pallas as pl
from jax.experimental.pallas import tpu as pltpu
from jax.sharding import PartitionSpec as P

HD = 128


norm_epsilon = 1e-05


def row_norm(rows, gain):
    widened = rows.astype(jnp.float32)
    return (
        widened
        * lax.rsqrt(jnp.mean(widened * widened, axis=1, keepdims=True) + norm_epsilon)
        * gain
    ).astype(jnp.bfloat16)


def attention_kernel(heads, length_ref, normed_ref, values_w_ref, probe_ref, out_ref):
    normed = normed_ref[...]
    seq_len = normed.shape[0]
    values = jnp.dot(normed, values_w_ref[...], preferred_element_type=jnp.float32).astype(
        jnp.bfloat16
    )
    probe = probe_ref[...]
    probe_high = probe.astype(jnp.bfloat16)
    probe_low = (probe - probe_high.astype(jnp.float32)).astype(jnp.bfloat16)
    contract = (((1,), (1,)), ((), ()))
    scores = lax.dot_general(
        probe_high, normed, contract, preferred_element_type=jnp.float32
    ) + lax.dot_general(probe_low, normed, contract, preferred_element_type=jnp.float32)
    scores = scores / math.sqrt(HD)
    live = lax.broadcasted_iota(jnp.int32, (heads, seq_len), 1) < length_ref[0]
    scores = jnp.where(live, scores, -jnp.inf)
    peak = jnp.max(scores, axis=1, keepdims=True)
    shifted = jnp.exp(scores - peak)
    weights = (shifted / jnp.sum(shifted, axis=1, keepdims=True)).astype(jnp.bfloat16)
    mixed = jnp.dot(weights, values, preferred_element_type=jnp.float32)
    for head in range(heads):
        block = slice(head * HD, (head + 1) * HD)
        out_ref[:, block] = mixed[head : head + 1, block].astype(out_ref.dtype)


def attend(length, normed, values_w, probe):
    heads = probe.shape[0]
    seq_len, width = normed.shape
    columns = values_w.shape[1]
    flops = 2 * seq_len * width * columns + 4 * heads * seq_len * width + 2 * heads * seq_len * columns
    return pl.pallas_call(
        functools.partial(attention_kernel, heads),
        out_shape=jax.ShapeDtypeStruct((1, columns), jnp.bfloat16),
        in_specs=[
            pl.BlockSpec(memory_space=pltpu.SMEM),
            pl.BlockSpec(memory_space=pltpu.VMEM),
            pl.BlockSpec(memory_space=pltpu.VMEM),
            pl.BlockSpec(memory_space=pltpu.VMEM),
        ],
        out_specs=pl.BlockSpec(memory_space=pltpu.VMEM),
        cost_estimate=pl.CostEstimate(
            flops=flops,
            bytes_accessed=2 * seq_len * width + 2 * width * columns + 4 * heads * width,
            transcendentals=heads * seq_len,
        ),
    )(length, normed, values_w, probe)


def exchange(rows, axis_name):
    return lax.all_to_all(rows, axis_name, split_axis=0, concat_axis=0, tiled=True)


def gather_by_exchange(piece, axis_name, count):
    spread = jnp.broadcast_to(piece[None], (count,) + piece.shape)
    return exchange(spread, axis_name)


def select_rows(selector, rows):
    return jnp.dot(
        selector.astype(jnp.bfloat16), rows, preferred_element_type=jnp.float32
    ).astype(jnp.bfloat16)


def local(
    text_embeds,
    vision_tokens,
    vision_request,
    image_start,
    lengths,
    attn_gain,
    w_query,
    w_key,
    w_value,
    w_out,
    final_gain,
    lm_head,
):
    groups = lax.axis_size("fsdp")
    seq_count = lax.axis_size("seq")
    seq_index = lax.axis_index("seq")
    seq_len = text_embeds.shape[0]
    width = text_embeds.shape[1]
    columns = w_key.shape[1]
    heads_local = columns // HD
    dpiece = width // groups
    quarter = groups // seq_count
    capacity = max(2, 2 * vision_tokens.shape[0] // groups)
    last_index = lengths[0] - 1

    destination = vision_request[:, 0]
    onehot = (destination[:, None] == jnp.arange(groups, dtype=jnp.int32)[None, :]).astype(
        jnp.int32
    )
    slot_index = jnp.sum((jnp.cumsum(onehot, axis=0) - onehot) * onehot, axis=1)
    counts = jnp.sum(onehot, axis=0)

    final_text = lax.dynamic_slice_in_dim(text_embeds, last_index, 1, 0)
    last_normed = row_norm(final_text, attn_gain)
    pieces = jnp.stack(
        [
            final_text.reshape(groups, dpiece),
            last_normed.reshape(groups, dpiece),
            jnp.broadcast_to(counts.astype(jnp.bfloat16)[:, None], (groups, dpiece)),
        ],
        axis=1,
    )
    pieces_in = exchange(pieces, "fsdp")
    text_part = pieces_in[:, 0]
    normed_part = pieces_in[:, 1]
    arrived = pieces_in[:, 2, :1].astype(jnp.int32)

    query_partial = jnp.dot(normed_part, w_query, preferred_element_type=jnp.float32)
    query_mine = jnp.sum(exchange(query_partial, "fsdp"), axis=0).astype(jnp.bfloat16)
    query_all = gather_by_exchange(query_mine, "fsdp", groups)

    query_heads = query_all.astype(jnp.float32).reshape(groups, heads_local, HD)
    key_rows = w_key.astype(jnp.float32).reshape(dpiece, heads_local, HD)
    probe_part = jnp.einsum(
        "rhc,dhc->rhd", query_heads, key_rows, precision=lax.Precision.HIGHEST
    )
    probe_in = exchange(probe_part, "fsdp")
    probe = jnp.transpose(probe_in, (1, 0, 2)).reshape(heads_local, width)

    full_vision = lax.all_gather(vision_tokens, "seq", axis=1, tiled=True)
    slot_of = destination * capacity + slot_index
    outbox_select = (
        jnp.arange(groups * capacity, dtype=jnp.int32)[:, None] == slot_of[None, :]
    )
    outbox = select_rows(outbox_select, full_vision).reshape(groups, capacity, width)
    received = exchange(outbox, "fsdp")
    occupied = (
        (jnp.arange(capacity, dtype=jnp.int32)[None, :] < arrived).astype(jnp.int32).reshape(-1)
    )
    ranking = jnp.cumsum(occupied) - occupied
    positions = jnp.where(occupied > 0, image_start[0] + ranking, seq_len)
    place = jnp.arange(seq_len, dtype=jnp.int32)[:, None] == positions[None, :]
    placed = select_rows(place, received.reshape(-1, width))
    replaced = jnp.any(place, axis=1, keepdims=True)
    states = jnp.where(replaced, placed, text_embeds)
    normed = row_norm(states, attn_gain)

    attended = attend(
        lengths, normed, lax.all_gather(w_value, "fsdp", axis=0, tiled=True), probe
    ).reshape(columns)

    attended_seq = gather_by_exchange(attended, "fsdp", groups)
    out_rows = lax.dynamic_slice_in_dim(w_out, seq_index * columns, columns, 0)
    partial_out = jnp.dot(attended_seq, out_rows, preferred_element_type=jnp.float32)
    out_mine = lax.psum_scatter(partial_out, "seq", scatter_dimension=0, tiled=True)
    text_mine = lax.dynamic_slice_in_dim(text_part, seq_index * quarter, quarter, 0)
    residual_out = text_mine.astype(jnp.float32) + out_mine
    gain_part = lax.dynamic_slice_in_dim(final_gain, lax.axis_index("fsdp") * dpiece, dpiece, 0)
    scaled_part = (residual_out * gain_part[None, :]).astype(jnp.bfloat16)
    square_part = jnp.sum(residual_out * residual_out, axis=1, keepdims=True)
    square_high = square_part.astype(jnp.bfloat16)
    square_low = (square_part - square_high.astype(jnp.float32)).astype(jnp.bfloat16)
    payload = jnp.concatenate([scaled_part, square_high, square_low], axis=1)
    payload_all = gather_by_exchange(payload, "fsdp", groups)
    scaled_out = jnp.transpose(payload_all[:, :, :dpiece], (1, 0, 2)).reshape(quarter, width)
    square_sum = jnp.sum(
        payload_all[:, :, dpiece:].astype(jnp.float32), axis=(0, 2)
    )
    mean_square = square_sum / width
    logits = jnp.dot(scaled_out, lm_head, preferred_element_type=jnp.float32)
    local_max = jnp.max(logits, axis=1) * lax.rsqrt(mean_square + norm_epsilon)
    max_all = gather_by_exchange(local_max, "fsdp", groups)
    max_logit = jnp.max(max_all, axis=0)
    return (jnp.sqrt(mean_square), max_logit)


def solution(mesh):
    return jax.shard_map(
        local,
        mesh=mesh,
        in_specs=(
            P("fsdp", None),
            P("fsdp", "seq"),
            P("fsdp", None),
            P("fsdp"),
            P("fsdp"),
            P(),
            P("fsdp", "seq"),
            P("fsdp", "seq"),
            P("fsdp", "seq"),
            P(None, "fsdp"),
            P(),
            P(None, "fsdp"),
        ),
        out_specs=(P("seq"), P("seq")),
        check_vma=False,
    )
```

```python
import math

import jax
import jax.numpy as jnp
from jax import lax
from jax.sharding import PartitionSpec as P

HD = 128


norm_epsilon = 1e-05


def row_norm(rows, gain):
    widened = rows.astype(jnp.float32)
    return (
        widened
        * lax.rsqrt(jnp.mean(widened * widened, axis=1, keepdims=True) + norm_epsilon)
        * gain
    ).astype(jnp.bfloat16)


def exchange(rows, axis_name):
    return lax.all_to_all(rows, axis_name, split_axis=0, concat_axis=0, tiled=True)


def gather_by_exchange(piece, axis_name, count):
    spread = jnp.broadcast_to(piece[None], (count,) + piece.shape)
    return exchange(spread, axis_name)


def select_rows(selector, rows):
    return jnp.dot(
        selector.astype(jnp.bfloat16), rows, preferred_element_type=jnp.float32
    ).astype(jnp.bfloat16)


def local(
    text_embeds,
    vision_tokens,
    vision_request,
    image_start,
    lengths,
    attn_gain,
    w_query,
    w_key,
    w_value,
    w_out,
    final_gain,
    lm_head,
):
    groups = lax.axis_size("fsdp")
    seq_count = lax.axis_size("seq")
    seq_index = lax.axis_index("seq")
    seq_len = text_embeds.shape[0]
    width = text_embeds.shape[1]
    columns = w_key.shape[1]
    heads_local = columns // HD
    dpiece = width // groups
    quarter = groups // seq_count
    capacity = max(2, 2 * vision_tokens.shape[0] // groups)
    last_index = lengths[0] - 1

    destination = vision_request[:, 0]
    onehot = (destination[:, None] == jnp.arange(groups, dtype=jnp.int32)[None, :]).astype(
        jnp.int32
    )
    slot_index = jnp.sum((jnp.cumsum(onehot, axis=0) - onehot) * onehot, axis=1)
    counts = jnp.sum(onehot, axis=0)

    final_text = lax.dynamic_slice_in_dim(text_embeds, last_index, 1, 0)
    last_normed = row_norm(final_text, attn_gain)
    pieces = jnp.stack(
        [
            final_text.reshape(groups, dpiece),
            last_normed.reshape(groups, dpiece),
            jnp.broadcast_to(counts.astype(jnp.bfloat16)[:, None], (groups, dpiece)),
        ],
        axis=1,
    )
    pieces_in = exchange(pieces, "fsdp")
    text_part = pieces_in[:, 0]
    normed_part = pieces_in[:, 1]
    arrived = pieces_in[:, 2, :1].astype(jnp.int32)

    query_partial = jnp.dot(normed_part, w_query, preferred_element_type=jnp.float32)
    query_mine = jnp.sum(exchange(query_partial, "fsdp"), axis=0).astype(jnp.bfloat16)
    query_all = gather_by_exchange(query_mine, "fsdp", groups)

    query_heads = query_all.astype(jnp.float32).reshape(groups, heads_local, HD)
    key_rows = w_key.astype(jnp.float32).reshape(dpiece, heads_local, HD)
    probe_part = jnp.einsum(
        "rhc,dhc->rhd", query_heads, key_rows, precision=lax.Precision.HIGHEST
    )
    probe_in = exchange(probe_part, "fsdp")
    probe = jnp.transpose(probe_in, (1, 0, 2)).reshape(heads_local, width)

    piece_width = vision_tokens.shape[1]
    slot_of = destination * capacity + slot_index
    outbox_select = (
        jnp.arange(groups * capacity, dtype=jnp.int32)[:, None] == slot_of[None, :]
    )
    outbox = select_rows(outbox_select, vision_tokens).reshape(groups, capacity, piece_width)
    received_piece = exchange(outbox, "fsdp").reshape(groups * capacity, piece_width)
    received_all = gather_by_exchange(received_piece, "seq", seq_count)
    received = jnp.transpose(received_all, (1, 0, 2)).reshape(groups * capacity, width)
    occupied = (
        (jnp.arange(capacity, dtype=jnp.int32)[None, :] < arrived).astype(jnp.int32).reshape(-1)
    )
    ranking = jnp.cumsum(occupied) - occupied
    positions = jnp.where(occupied > 0, image_start[0] + ranking, seq_len)
    place = jnp.arange(seq_len, dtype=jnp.int32)[:, None] == positions[None, :]
    placed = select_rows(place, received.reshape(-1, width))
    replaced = jnp.any(place, axis=1, keepdims=True)
    states = jnp.where(replaced, placed, text_embeds)
    normed = row_norm(states, attn_gain)

    value_sum = jnp.dot(
        normed,
        lax.all_gather(w_value, "fsdp", axis=0, tiled=True),
        preferred_element_type=jnp.float32,
    )
    value_heads = value_sum.astype(jnp.bfloat16).reshape(seq_len, heads_local, HD)
    scores = jnp.dot(
        normed.astype(jnp.float32), probe.T, precision=lax.Precision.HIGHEST
    ).T / math.sqrt(HD)
    live_keys = jnp.arange(seq_len, dtype=jnp.int32) < lengths[0]
    scores = jnp.where(live_keys[None, :], scores, -jnp.inf)
    peak = jnp.max(scores, axis=1, keepdims=True)
    shifted = jnp.exp(scores - peak)
    weights = (shifted / jnp.sum(shifted, axis=1, keepdims=True)).astype(jnp.bfloat16)
    attended = (
        jnp.einsum("hj,jhc->hc", weights, value_heads, preferred_element_type=jnp.float32)
        .astype(jnp.bfloat16)
        .reshape(columns)
    )

    attended_seq = gather_by_exchange(attended, "fsdp", groups)
    out_rows = lax.dynamic_slice_in_dim(w_out, seq_index * columns, columns, 0)
    partial_out = jnp.dot(attended_seq, out_rows, preferred_element_type=jnp.float32)
    out_mine = lax.psum_scatter(partial_out, "seq", scatter_dimension=0, tiled=True)
    text_mine = lax.dynamic_slice_in_dim(text_part, seq_index * quarter, quarter, 0)
    residual_out = text_mine.astype(jnp.float32) + out_mine
    gain_part = lax.dynamic_slice_in_dim(final_gain, lax.axis_index("fsdp") * dpiece, dpiece, 0)
    scaled_part = (residual_out * gain_part[None, :]).astype(jnp.bfloat16)
    square_part = jnp.sum(residual_out * residual_out, axis=1, keepdims=True)
    square_high = square_part.astype(jnp.bfloat16)
    square_low = (square_part - square_high.astype(jnp.float32)).astype(jnp.bfloat16)
    payload = jnp.concatenate([scaled_part, square_high, square_low], axis=1)
    payload_all = gather_by_exchange(payload, "fsdp", groups)
    scaled_out = jnp.transpose(payload_all[:, :, :dpiece], (1, 0, 2)).reshape(quarter, width)
    square_sum = jnp.sum(
        payload_all[:, :, dpiece:].astype(jnp.float32), axis=(0, 2)
    )
    mean_square = square_sum / width
    logits = jnp.dot(scaled_out, lm_head, preferred_element_type=jnp.float32)
    local_max = jnp.max(logits, axis=1) * lax.rsqrt(mean_square + norm_epsilon)
    max_all = gather_by_exchange(local_max, "fsdp", groups)
    max_logit = jnp.max(max_all, axis=0)
    return (jnp.sqrt(mean_square), max_logit)


def solution(mesh):
    return jax.shard_map(
        local,
        mesh=mesh,
        in_specs=(
            P("fsdp", None),
            P("fsdp", "seq"),
            P("fsdp", None),
            P("fsdp"),
            P("fsdp"),
            P(),
            P("fsdp", "seq"),
            P("fsdp", "seq"),
            P("fsdp", "seq"),
            P(None, "fsdp"),
            P(),
            P(None, "fsdp"),
        ),
        out_specs=(P("seq"), P("seq")),
        check_vma=False,
    )
```

```python
import math

import jax
import jax.numpy as jnp
from jax import lax
from jax.sharding import PartitionSpec as P

HD = 128


norm_epsilon = 1e-05


def row_norm(rows, gain):
    widened = rows.astype(jnp.float32)
    return (
        widened
        * lax.rsqrt(jnp.mean(widened * widened, axis=1, keepdims=True) + norm_epsilon)
        * gain
    ).astype(jnp.bfloat16)


def exchange(rows, axis_name):
    return lax.all_to_all(rows, axis_name, split_axis=0, concat_axis=0, tiled=True)


def gather_by_exchange(piece, axis_name, count):
    spread = jnp.broadcast_to(piece[None], (count,) + piece.shape)
    return exchange(spread, axis_name)


def select_rows(selector, rows):
    return jnp.dot(
        selector.astype(jnp.bfloat16), rows, preferred_element_type=jnp.float32
    ).astype(jnp.bfloat16)


def local(
    text_embeds,
    vision_tokens,
    vision_request,
    image_start,
    lengths,
    attn_gain,
    w_query,
    w_key,
    w_value,
    w_out,
    final_gain,
    lm_head,
):
    groups = lax.axis_size("fsdp")
    seq_count = lax.axis_size("seq")
    seq_index = lax.axis_index("seq")
    seq_len = text_embeds.shape[0]
    width = text_embeds.shape[1]
    columns = w_key.shape[1]
    heads_local = columns // HD
    dpiece = width // groups
    quarter = groups // seq_count
    capacity = max(2, 2 * vision_tokens.shape[0] // groups)
    last_index = lengths[0] - 1

    destination = vision_request[:, 0]
    onehot = (destination[:, None] == jnp.arange(groups, dtype=jnp.int32)[None, :]).astype(
        jnp.int32
    )
    slot_index = jnp.sum((jnp.cumsum(onehot, axis=0) - onehot) * onehot, axis=1)
    counts = jnp.sum(onehot, axis=0)

    final_text = lax.dynamic_slice_in_dim(text_embeds, last_index, 1, 0)
    last_normed = row_norm(final_text, attn_gain)
    pieces = jnp.stack(
        [
            final_text.reshape(groups, dpiece),
            last_normed.reshape(groups, dpiece),
            jnp.broadcast_to(counts.astype(jnp.bfloat16)[:, None], (groups, dpiece)),
        ],
        axis=1,
    )
    pieces_in = exchange(pieces, "fsdp")
    text_part = pieces_in[:, 0]
    normed_part = pieces_in[:, 1]
    arrived = pieces_in[:, 2, :1].astype(jnp.int32)

    query_partial = jnp.dot(normed_part, w_query, preferred_element_type=jnp.float32)
    query_mine = jnp.sum(exchange(query_partial, "fsdp"), axis=0).astype(jnp.bfloat16)
    query_all = gather_by_exchange(query_mine, "fsdp", groups)

    query_heads = query_all.astype(jnp.float32).reshape(groups, heads_local, HD)
    key_rows = w_key.astype(jnp.float32).reshape(dpiece, heads_local, HD)
    probe_part = jnp.einsum(
        "rhc,dhc->rhd", query_heads, key_rows, precision=lax.Precision.HIGHEST
    )
    probe_in = exchange(probe_part, "fsdp")
    probe = jnp.transpose(probe_in, (1, 0, 2)).reshape(heads_local, width)

    piece_width = vision_tokens.shape[1]
    slot_of = destination * capacity + slot_index
    outbox_select = (
        jnp.arange(groups * capacity, dtype=jnp.int32)[:, None] == slot_of[None, :]
    )
    outbox = select_rows(outbox_select, vision_tokens).reshape(groups, capacity, piece_width)
    received_piece = exchange(outbox, "fsdp").reshape(groups * capacity, piece_width)
    received = lax.all_gather(received_piece, "seq", axis=1, tiled=True)
    occupied = (
        (jnp.arange(capacity, dtype=jnp.int32)[None, :] < arrived).astype(jnp.int32).reshape(-1)
    )
    ranking = jnp.cumsum(occupied) - occupied
    positions = jnp.where(occupied > 0, image_start[0] + ranking, seq_len)
    place = jnp.arange(seq_len, dtype=jnp.int32)[:, None] == positions[None, :]
    placed = select_rows(place, received.reshape(-1, width))
    replaced = jnp.any(place, axis=1, keepdims=True)
    states = jnp.where(replaced, placed, text_embeds)
    normed = row_norm(states, attn_gain)

    value_sum = jnp.dot(
        normed,
        lax.all_gather(w_value, "fsdp", axis=0, tiled=True),
        preferred_element_type=jnp.float32,
    )
    value_heads = value_sum.astype(jnp.bfloat16).reshape(seq_len, heads_local, HD)
    scores = jnp.dot(
        normed.astype(jnp.float32), probe.T, precision=lax.Precision.HIGHEST
    ).T / math.sqrt(HD)
    live_keys = jnp.arange(seq_len, dtype=jnp.int32) < lengths[0]
    scores = jnp.where(live_keys[None, :], scores, -jnp.inf)
    peak = jnp.max(scores, axis=1, keepdims=True)
    shifted = jnp.exp(scores - peak)
    weights = (shifted / jnp.sum(shifted, axis=1, keepdims=True)).astype(jnp.bfloat16)
    attended = (
        jnp.einsum("hj,jhc->hc", weights, value_heads, preferred_element_type=jnp.float32)
        .astype(jnp.bfloat16)
        .reshape(columns)
    )

    attended_seq = gather_by_exchange(attended, "fsdp", groups)
    out_rows = lax.dynamic_slice_in_dim(w_out, seq_index * columns, columns, 0)
    partial_out = jnp.dot(attended_seq, out_rows, preferred_element_type=jnp.float32)
    out_mine = lax.psum_scatter(partial_out, "seq", scatter_dimension=0, tiled=True)
    text_mine = lax.dynamic_slice_in_dim(text_part, seq_index * quarter, quarter, 0)
    residual_out = text_mine.astype(jnp.float32) + out_mine
    gain_part = lax.dynamic_slice_in_dim(final_gain, lax.axis_index("fsdp") * dpiece, dpiece, 0)
    scaled_part = (residual_out * gain_part[None, :]).astype(jnp.bfloat16)
    square_part = jnp.sum(residual_out * residual_out, axis=1, keepdims=True)
    square_high = square_part.astype(jnp.bfloat16)
    square_low = (square_part - square_high.astype(jnp.float32)).astype(jnp.bfloat16)
    payload = jnp.concatenate([scaled_part, square_high, square_low], axis=1)
    payload_all = gather_by_exchange(payload, "fsdp", groups)
    scaled_out = jnp.transpose(payload_all[:, :, :dpiece], (1, 0, 2)).reshape(quarter, width)
    square_sum = jnp.sum(
        payload_all[:, :, dpiece:].astype(jnp.float32), axis=(0, 2)
    )
    mean_square = square_sum / width
    logits = jnp.dot(scaled_out, lm_head, preferred_element_type=jnp.float32)
    local_max = jnp.max(logits, axis=1) * lax.rsqrt(mean_square + norm_epsilon)
    max_all = gather_by_exchange(local_max, "fsdp", groups)
    max_logit = jnp.max(max_all, axis=0)
    return (jnp.sqrt(mean_square), max_logit)


def solution(mesh):
    return jax.shard_map(
        local,
        mesh=mesh,
        in_specs=(
            P("fsdp", None),
            P("fsdp", "seq"),
            P("fsdp", None),
            P("fsdp"),
            P("fsdp"),
            P(),
            P("fsdp", "seq"),
            P("fsdp", "seq"),
            P("fsdp", "seq"),
            P(None, "fsdp"),
            P(),
            P(None, "fsdp"),
        ),
        out_specs=(P("seq"), P("seq")),
        check_vma=False,
    )
```

```python
import math

import jax
import jax.numpy as jnp
from jax import lax
from jax.sharding import PartitionSpec as P

HD = 128


norm_epsilon = 1e-05


def row_norm(rows, gain):
    widened = rows.astype(jnp.float32)
    return (
        widened
        * lax.rsqrt(jnp.mean(widened * widened, axis=1, keepdims=True) + norm_epsilon)
        * gain
    ).astype(jnp.bfloat16)


def exchange(rows, axis_name):
    return lax.all_to_all(rows, axis_name, split_axis=0, concat_axis=0, tiled=True)


def gather_by_exchange(piece, axis_name, count):
    spread = jnp.broadcast_to(piece[None], (count,) + piece.shape)
    return exchange(spread, axis_name)


def select_rows(selector, rows):
    return jnp.dot(
        selector.astype(jnp.bfloat16), rows, preferred_element_type=jnp.float32
    ).astype(jnp.bfloat16)


def local(
    text_embeds,
    vision_tokens,
    vision_request,
    image_start,
    lengths,
    attn_gain,
    w_query,
    w_key,
    w_value,
    w_out,
    final_gain,
    lm_head,
):
    groups = lax.axis_size("fsdp")
    seq_count = lax.axis_size("seq")
    seq_index = lax.axis_index("seq")
    seq_len = text_embeds.shape[0]
    width = text_embeds.shape[1]
    columns = w_key.shape[1]
    heads_local = columns // HD
    dpiece = width // groups
    quarter = groups // seq_count
    capacity = max(2, 2 * vision_tokens.shape[0] // groups)
    last_index = lengths[0] - 1

    destination = vision_request[:, 0]
    onehot = (destination[:, None] == jnp.arange(groups, dtype=jnp.int32)[None, :]).astype(
        jnp.int32
    )
    slot_index = jnp.sum((jnp.cumsum(onehot, axis=0) - onehot) * onehot, axis=1)
    counts = jnp.sum(onehot, axis=0)

    final_text = lax.dynamic_slice_in_dim(text_embeds, last_index, 1, 0)
    last_normed = row_norm(final_text, attn_gain)
    pieces = jnp.stack(
        [
            final_text.reshape(groups, dpiece),
            last_normed.reshape(groups, dpiece),
            jnp.broadcast_to(counts.astype(jnp.bfloat16)[:, None], (groups, dpiece)),
        ],
        axis=1,
    )
    pieces_in = exchange(pieces, "fsdp")
    text_part = pieces_in[:, 0]
    normed_part = pieces_in[:, 1]
    arrived = pieces_in[:, 2, :1].astype(jnp.int32)

    query_partial = jnp.dot(normed_part, w_query, preferred_element_type=jnp.float32)
    query_mine = jnp.sum(exchange(query_partial, "fsdp"), axis=0).astype(jnp.bfloat16)
    query_all = gather_by_exchange(query_mine, "fsdp", groups)

    query_heads = query_all.astype(jnp.float32).reshape(groups, heads_local, HD)
    key_rows = w_key.astype(jnp.float32).reshape(dpiece, heads_local, HD)
    probe_part = jnp.einsum(
        "rhc,dhc->rhd", query_heads, key_rows, precision=lax.Precision.HIGHEST
    )
    probe_in = exchange(probe_part, "fsdp")
    probe = jnp.transpose(probe_in, (1, 0, 2)).reshape(heads_local, width)

    piece_width = vision_tokens.shape[1]
    slot_of = destination * capacity + slot_index
    outbox_select = (
        jnp.arange(groups * capacity, dtype=jnp.int32)[:, None] == slot_of[None, :]
    )
    outbox = select_rows(outbox_select, vision_tokens).reshape(groups, capacity, piece_width)
    received_piece = exchange(outbox, "fsdp").reshape(groups * capacity, piece_width)
    received_all = gather_by_exchange(received_piece, "seq", seq_count)
    received = jnp.transpose(received_all, (1, 0, 2)).reshape(groups * capacity, width)
    occupied = (
        (jnp.arange(capacity, dtype=jnp.int32)[None, :] < arrived).astype(jnp.int32).reshape(-1)
    )
    ranking = jnp.cumsum(occupied) - occupied
    positions = jnp.where(occupied > 0, image_start[0] + ranking, seq_len)
    place = jnp.arange(seq_len, dtype=jnp.int32)[:, None] == positions[None, :]
    placed = select_rows(place, received.reshape(-1, width))
    replaced = jnp.any(place, axis=1, keepdims=True)
    states = jnp.where(replaced, placed, text_embeds)
    normed = row_norm(states, attn_gain)

    value_sum = jnp.dot(
        normed,
        lax.all_gather(w_value, "fsdp", axis=0, tiled=True),
        preferred_element_type=jnp.float32,
    )
    value_heads = value_sum.astype(jnp.bfloat16).reshape(seq_len, heads_local, HD)
    scores = jnp.dot(
        normed.astype(jnp.float32), probe.T, precision=lax.Precision.HIGHEST
    ).T / math.sqrt(HD)
    live_keys = jnp.arange(seq_len, dtype=jnp.int32) < lengths[0]
    scores = jnp.where(live_keys[None, :], scores, -jnp.inf)
    peak = jnp.max(scores, axis=1, keepdims=True)
    shifted = jnp.exp(scores - peak)
    weights = (shifted / jnp.sum(shifted, axis=1, keepdims=True)).astype(jnp.bfloat16)
    attended = (
        jnp.einsum("hj,jhc->hc", weights, value_heads, preferred_element_type=jnp.float32)
        .astype(jnp.bfloat16)
        .reshape(columns)
    )

    attended_seq = gather_by_exchange(attended, "fsdp", groups)
    out_rows = lax.dynamic_slice_in_dim(w_out, seq_index * columns, columns, 0)
    partial_out = jnp.dot(attended_seq, out_rows, preferred_element_type=jnp.float32)
    out_mine = lax.psum_scatter(partial_out, "seq", scatter_dimension=0, tiled=True)
    text_mine = lax.dynamic_slice_in_dim(text_part, seq_index * quarter, quarter, 0)
    residual_out = text_mine.astype(jnp.float32) + out_mine
    gain_part = lax.dynamic_slice_in_dim(final_gain, lax.axis_index("fsdp") * dpiece, dpiece, 0)
    scaled_part = (residual_out * gain_part[None, :]).astype(jnp.bfloat16)
    square_part = jnp.sum(residual_out * residual_out, axis=1, keepdims=True)
    square_high = square_part.astype(jnp.bfloat16)
    square_low = (square_part - square_high.astype(jnp.float32)).astype(jnp.bfloat16)
    payload = jnp.concatenate([scaled_part, square_high, square_low], axis=1)
    payload_all = gather_by_exchange(payload.reshape(-1), "fsdp", groups).reshape(
        (groups,) + payload.shape
    )
    scaled_out = jnp.transpose(payload_all[:, :, :dpiece], (1, 0, 2)).reshape(quarter, width)
    square_sum = jnp.sum(
        payload_all[:, :, dpiece:].astype(jnp.float32), axis=(0, 2)
    )
    mean_square = square_sum / width
    logits = jnp.dot(scaled_out, lm_head, preferred_element_type=jnp.float32)
    local_max = jnp.max(logits, axis=1) * lax.rsqrt(mean_square + norm_epsilon)
    max_all = gather_by_exchange(local_max, "fsdp", groups)
    max_logit = jnp.max(max_all, axis=0)
    return (jnp.sqrt(mean_square), max_logit)


def solution(mesh):
    return jax.shard_map(
        local,
        mesh=mesh,
        in_specs=(
            P("fsdp", None),
            P("fsdp", "seq"),
            P("fsdp", None),
            P("fsdp"),
            P("fsdp"),
            P(),
            P("fsdp", "seq"),
            P("fsdp", "seq"),
            P("fsdp", "seq"),
            P(None, "fsdp"),
            P(),
            P(None, "fsdp"),
        ),
        out_specs=(P("seq"), P("seq")),
        check_vma=False,
    )
```

```python
import math

import jax
import jax.numpy as jnp
from jax import lax
from jax.sharding import PartitionSpec as P

HD = 128


norm_epsilon = 1e-05


def row_norm(rows, gain):
    widened = rows.astype(jnp.float32)
    return (
        widened
        * lax.rsqrt(jnp.mean(widened * widened, axis=1, keepdims=True) + norm_epsilon)
        * gain
    ).astype(jnp.bfloat16)


def exchange(rows, axis_name):
    return lax.all_to_all(rows, axis_name, split_axis=0, concat_axis=0, tiled=True)


def gather_by_exchange(piece, axis_name, count):
    spread = jnp.broadcast_to(piece[None], (count,) + piece.shape)
    return exchange(spread, axis_name)


def select_rows(selector, rows):
    return jnp.dot(
        selector.astype(jnp.bfloat16), rows, preferred_element_type=jnp.float32
    ).astype(jnp.bfloat16)


def local(
    text_embeds,
    vision_tokens,
    vision_request,
    image_start,
    lengths,
    attn_gain,
    w_query,
    w_key,
    w_value,
    w_out,
    final_gain,
    lm_head,
):
    groups = lax.axis_size("fsdp")
    seq_count = lax.axis_size("seq")
    seq_index = lax.axis_index("seq")
    seq_len = text_embeds.shape[0]
    width = text_embeds.shape[1]
    columns = w_key.shape[1]
    heads_local = columns // HD
    dpiece = width // groups
    quarter = groups // seq_count
    capacity = max(2, 2 * vision_tokens.shape[0] // groups)
    last_index = lengths[0] - 1

    destination = vision_request[:, 0]
    onehot = (destination[:, None] == jnp.arange(groups, dtype=jnp.int32)[None, :]).astype(
        jnp.int32
    )
    slot_index = jnp.sum((jnp.cumsum(onehot, axis=0) - onehot) * onehot, axis=1)
    counts = jnp.sum(onehot, axis=0)

    final_text = lax.dynamic_slice_in_dim(text_embeds, last_index, 1, 0)
    last_normed = row_norm(final_text, attn_gain)
    pieces = jnp.stack(
        [
            final_text.reshape(groups, dpiece),
            last_normed.reshape(groups, dpiece),
            jnp.broadcast_to(counts.astype(jnp.bfloat16)[:, None], (groups, dpiece)),
        ],
        axis=1,
    )
    pieces_in = exchange(pieces, "fsdp")
    text_part = pieces_in[:, 0]
    normed_part = pieces_in[:, 1]
    arrived = pieces_in[:, 2, :1].astype(jnp.int32)

    query_partial = jnp.dot(normed_part, w_query, preferred_element_type=jnp.float32)
    query_mine = jnp.sum(exchange(query_partial, "fsdp"), axis=0).astype(jnp.bfloat16)
    value_weights = lax.all_gather(w_value, "fsdp", axis=0, tiled=True)
    query_mine, value_weights = lax.optimization_barrier((query_mine, value_weights))
    query_all = gather_by_exchange(query_mine, "fsdp", groups)

    query_heads = query_all.astype(jnp.float32).reshape(groups, heads_local, HD)
    key_rows = w_key.astype(jnp.float32).reshape(dpiece, heads_local, HD)
    probe_part = jnp.einsum(
        "rhc,dhc->rhd", query_heads, key_rows, precision=lax.Precision.HIGHEST
    )
    probe_in = exchange(probe_part, "fsdp")
    probe = jnp.transpose(probe_in, (1, 0, 2)).reshape(heads_local, width)

    piece_width = vision_tokens.shape[1]
    slot_of = destination * capacity + slot_index
    outbox_select = (
        jnp.arange(groups * capacity, dtype=jnp.int32)[:, None] == slot_of[None, :]
    )
    outbox = select_rows(outbox_select, vision_tokens).reshape(groups, capacity, piece_width)
    received_piece = exchange(outbox, "fsdp").reshape(groups * capacity, piece_width)
    received = lax.all_gather(received_piece, "seq", axis=1, tiled=True)
    occupied = (
        (jnp.arange(capacity, dtype=jnp.int32)[None, :] < arrived).astype(jnp.int32).reshape(-1)
    )
    ranking = jnp.cumsum(occupied) - occupied
    positions = jnp.where(occupied > 0, image_start[0] + ranking, seq_len)
    place = jnp.arange(seq_len, dtype=jnp.int32)[:, None] == positions[None, :]
    placed = select_rows(place, received.reshape(-1, width))
    replaced = jnp.any(place, axis=1, keepdims=True)
    states = jnp.where(replaced, placed, text_embeds)
    normed = row_norm(states, attn_gain)

    value_sum = jnp.dot(
        normed,
        value_weights,
        preferred_element_type=jnp.float32,
    )
    value_heads = value_sum.astype(jnp.bfloat16).reshape(seq_len, heads_local, HD)
    scores = jnp.dot(
        normed.astype(jnp.float32), probe.T, precision=lax.Precision.HIGHEST
    ).T / math.sqrt(HD)
    live_keys = jnp.arange(seq_len, dtype=jnp.int32) < lengths[0]
    scores = jnp.where(live_keys[None, :], scores, -jnp.inf)
    peak = jnp.max(scores, axis=1, keepdims=True)
    shifted = jnp.exp(scores - peak)
    weights = (shifted / jnp.sum(shifted, axis=1, keepdims=True)).astype(jnp.bfloat16)
    attended = (
        jnp.einsum("hj,jhc->hc", weights, value_heads, preferred_element_type=jnp.float32)
        .astype(jnp.bfloat16)
        .reshape(columns)
    )

    attended_seq = gather_by_exchange(attended, "fsdp", groups)
    out_rows = lax.dynamic_slice_in_dim(w_out, seq_index * columns, columns, 0)
    partial_out = jnp.dot(attended_seq, out_rows, preferred_element_type=jnp.float32)
    out_mine = lax.psum_scatter(partial_out, "seq", scatter_dimension=0, tiled=True)
    text_mine = lax.dynamic_slice_in_dim(text_part, seq_index * quarter, quarter, 0)
    residual_out = text_mine.astype(jnp.float32) + out_mine
    gain_part = lax.dynamic_slice_in_dim(final_gain, lax.axis_index("fsdp") * dpiece, dpiece, 0)
    scaled_part = (residual_out * gain_part[None, :]).astype(jnp.bfloat16)
    square_part = jnp.sum(residual_out * residual_out, axis=1, keepdims=True)
    square_high = square_part.astype(jnp.bfloat16)
    square_low = (square_part - square_high.astype(jnp.float32)).astype(jnp.bfloat16)
    payload = jnp.concatenate([scaled_part, square_high, square_low], axis=1)
    payload_all = gather_by_exchange(payload, "fsdp", groups)
    scaled_out = jnp.transpose(payload_all[:, :, :dpiece], (1, 0, 2)).reshape(quarter, width)
    square_sum = jnp.sum(
        payload_all[:, :, dpiece:].astype(jnp.float32), axis=(0, 2)
    )
    mean_square = square_sum / width
    logits = jnp.dot(scaled_out, lm_head, preferred_element_type=jnp.float32)
    local_max = jnp.max(logits, axis=1) * lax.rsqrt(mean_square + norm_epsilon)
    max_all = gather_by_exchange(local_max, "fsdp", groups)
    max_logit = jnp.max(max_all, axis=0)
    return (jnp.sqrt(mean_square), max_logit)


def solution(mesh):
    return jax.shard_map(
        local,
        mesh=mesh,
        in_specs=(
            P("fsdp", None),
            P("fsdp", "seq"),
            P("fsdp", None),
            P("fsdp"),
            P("fsdp"),
            P(),
            P("fsdp", "seq"),
            P("fsdp", "seq"),
            P("fsdp", "seq"),
            P(None, "fsdp"),
            P(),
            P(None, "fsdp"),
        ),
        out_specs=(P("seq"), P("seq")),
        check_vma=False,
    )
```

```python
import math

import jax
import jax.numpy as jnp
from jax import lax
from jax.sharding import PartitionSpec as P

HD = 128


norm_epsilon = 1e-05


def row_norm(rows, gain):
    widened = rows.astype(jnp.float32)
    return (
        widened
        * lax.rsqrt(jnp.mean(widened * widened, axis=1, keepdims=True) + norm_epsilon)
        * gain
    ).astype(jnp.bfloat16)


def exchange(rows, axis_name):
    return lax.all_to_all(rows, axis_name, split_axis=0, concat_axis=0, tiled=True)


def gather_by_exchange(piece, axis_name, count):
    spread = jnp.broadcast_to(piece[None], (count,) + piece.shape)
    return exchange(spread, axis_name)


def select_rows(selector, rows):
    return jnp.dot(
        selector.astype(jnp.bfloat16), rows, preferred_element_type=jnp.float32
    ).astype(jnp.bfloat16)


def local(
    text_embeds,
    vision_tokens,
    vision_request,
    image_start,
    lengths,
    attn_gain,
    w_query,
    w_key,
    w_value,
    w_out,
    final_gain,
    lm_head,
):
    groups = lax.axis_size("fsdp")
    seq_count = lax.axis_size("seq")
    seq_index = lax.axis_index("seq")
    seq_len = text_embeds.shape[0]
    width = text_embeds.shape[1]
    columns = w_key.shape[1]
    heads_local = columns // HD
    dpiece = width // groups
    quarter = groups // seq_count
    capacity = max(2, 2 * vision_tokens.shape[0] // groups)
    last_index = lengths[0] - 1

    destination = vision_request[:, 0]
    onehot = (destination[:, None] == jnp.arange(groups, dtype=jnp.int32)[None, :]).astype(
        jnp.int32
    )
    slot_index = jnp.sum((jnp.cumsum(onehot, axis=0) - onehot) * onehot, axis=1)
    counts = jnp.sum(onehot, axis=0)

    final_text = lax.dynamic_slice_in_dim(text_embeds, last_index, 1, 0)
    last_normed = row_norm(final_text, attn_gain)
    pieces = jnp.stack(
        [
            final_text.reshape(groups, dpiece),
            last_normed.reshape(groups, dpiece),
            jnp.broadcast_to(counts.astype(jnp.bfloat16)[:, None], (groups, dpiece)),
        ],
        axis=1,
    )
    pieces_in = exchange(pieces, "fsdp")
    text_part = pieces_in[:, 0]
    normed_part = pieces_in[:, 1]
    arrived = pieces_in[:, 2, :1].astype(jnp.int32)

    query_partial = jnp.dot(normed_part, w_query, preferred_element_type=jnp.float32)
    query_mine = jnp.sum(exchange(query_partial, "fsdp"), axis=0).astype(jnp.bfloat16)
    query_all = gather_by_exchange(query_mine, "fsdp", groups)

    query_heads = query_all.astype(jnp.float32).reshape(groups, heads_local, HD)
    key_rows = w_key.astype(jnp.float32).reshape(dpiece, heads_local, HD)
    probe_part = jnp.einsum(
        "rhc,dhc->rhd", query_heads, key_rows, precision=lax.Precision.HIGHEST
    )
    probe_flat = probe_part.reshape(groups, heads_local * dpiece)
    probe_high = probe_flat.astype(jnp.bfloat16)
    probe_low = (probe_flat - probe_high.astype(jnp.float32)).astype(jnp.bfloat16)

    piece_width = vision_tokens.shape[1]
    slot_of = destination * capacity + slot_index
    outbox_select = (
        jnp.arange(groups * capacity, dtype=jnp.int32)[:, None] == slot_of[None, :]
    )
    outbox = select_rows(outbox_select, vision_tokens).reshape(groups, capacity * piece_width)
    bundle = jnp.concatenate([outbox, probe_high, probe_low], axis=1)
    bundle_in = exchange(bundle, "fsdp")
    vision_end = capacity * piece_width
    probe_size = heads_local * dpiece
    received_piece = bundle_in[:, :vision_end].reshape(groups * capacity, piece_width)
    probe_in = (
        bundle_in[:, vision_end : vision_end + probe_size].astype(jnp.float32)
        + bundle_in[:, vision_end + probe_size :].astype(jnp.float32)
    ).reshape(groups, heads_local, dpiece)
    probe = jnp.transpose(probe_in, (1, 0, 2)).reshape(heads_local, width)
    received_all = gather_by_exchange(received_piece, "seq", seq_count)
    received = jnp.transpose(received_all, (1, 0, 2)).reshape(groups * capacity, width)
    occupied = (
        (jnp.arange(capacity, dtype=jnp.int32)[None, :] < arrived).astype(jnp.int32).reshape(-1)
    )
    ranking = jnp.cumsum(occupied) - occupied
    positions = jnp.where(occupied > 0, image_start[0] + ranking, seq_len)
    place = jnp.arange(seq_len, dtype=jnp.int32)[:, None] == positions[None, :]
    placed = select_rows(place, received.reshape(-1, width))
    replaced = jnp.any(place, axis=1, keepdims=True)
    states = jnp.where(replaced, placed, text_embeds)
    normed = row_norm(states, attn_gain)

    value_sum = jnp.dot(
        normed,
        lax.all_gather(w_value, "fsdp", axis=0, tiled=True),
        preferred_element_type=jnp.float32,
    )
    value_heads = value_sum.astype(jnp.bfloat16).reshape(seq_len, heads_local, HD)
    scores = jnp.dot(
        normed.astype(jnp.float32), probe.T, precision=lax.Precision.HIGHEST
    ).T / math.sqrt(HD)
    live_keys = jnp.arange(seq_len, dtype=jnp.int32) < lengths[0]
    scores = jnp.where(live_keys[None, :], scores, -jnp.inf)
    peak = jnp.max(scores, axis=1, keepdims=True)
    shifted = jnp.exp(scores - peak)
    weights = (shifted / jnp.sum(shifted, axis=1, keepdims=True)).astype(jnp.bfloat16)
    attended = (
        jnp.einsum("hj,jhc->hc", weights, value_heads, preferred_element_type=jnp.float32)
        .astype(jnp.bfloat16)
        .reshape(columns)
    )

    attended_seq = gather_by_exchange(attended, "fsdp", groups)
    out_rows = lax.dynamic_slice_in_dim(w_out, seq_index * columns, columns, 0)
    partial_out = jnp.dot(attended_seq, out_rows, preferred_element_type=jnp.float32)
    out_mine = lax.psum_scatter(partial_out, "seq", scatter_dimension=0, tiled=True)
    text_mine = lax.dynamic_slice_in_dim(text_part, seq_index * quarter, quarter, 0)
    residual_out = text_mine.astype(jnp.float32) + out_mine
    gain_part = lax.dynamic_slice_in_dim(final_gain, lax.axis_index("fsdp") * dpiece, dpiece, 0)
    scaled_part = (residual_out * gain_part[None, :]).astype(jnp.bfloat16)
    square_part = jnp.sum(residual_out * residual_out, axis=1, keepdims=True)
    square_high = square_part.astype(jnp.bfloat16)
    square_low = (square_part - square_high.astype(jnp.float32)).astype(jnp.bfloat16)
    payload = jnp.concatenate([scaled_part, square_high, square_low], axis=1)
    payload_all = gather_by_exchange(payload, "fsdp", groups)
    scaled_out = jnp.transpose(payload_all[:, :, :dpiece], (1, 0, 2)).reshape(quarter, width)
    square_sum = jnp.sum(
        payload_all[:, :, dpiece:].astype(jnp.float32), axis=(0, 2)
    )
    mean_square = square_sum / width
    logits = jnp.dot(scaled_out, lm_head, preferred_element_type=jnp.float32)
    local_max = jnp.max(logits, axis=1) * lax.rsqrt(mean_square + norm_epsilon)
    max_all = gather_by_exchange(local_max, "fsdp", groups)
    max_logit = jnp.max(max_all, axis=0)
    return (jnp.sqrt(mean_square), max_logit)


def solution(mesh):
    return jax.shard_map(
        local,
        mesh=mesh,
        in_specs=(
            P("fsdp", None),
            P("fsdp", "seq"),
            P("fsdp", None),
            P("fsdp"),
            P("fsdp"),
            P(),
            P("fsdp", "seq"),
            P("fsdp", "seq"),
            P("fsdp", "seq"),
            P(None, "fsdp"),
            P(),
            P(None, "fsdp"),
        ),
        out_specs=(P("seq"), P("seq")),
        check_vma=False,
    )
```

```python
import math

import jax
import jax.numpy as jnp
from jax import lax
from jax.sharding import PartitionSpec as P

HD = 128


norm_epsilon = 1e-05


def row_norm(rows, gain):
    widened = rows.astype(jnp.float32)
    return (
        widened
        * lax.rsqrt(jnp.mean(widened * widened, axis=1, keepdims=True) + norm_epsilon)
        * gain
    ).astype(jnp.bfloat16)


def exchange(rows, axis_name):
    return lax.all_to_all(rows, axis_name, split_axis=0, concat_axis=0, tiled=True)


def gather_by_exchange(piece, axis_name, count):
    spread = jnp.broadcast_to(piece[None], (count,) + piece.shape)
    return exchange(spread, axis_name)


def select_rows(selector, rows):
    return jnp.dot(
        selector.astype(jnp.bfloat16), rows, preferred_element_type=jnp.float32
    ).astype(jnp.bfloat16)


def local(
    text_embeds,
    vision_tokens,
    vision_request,
    image_start,
    lengths,
    attn_gain,
    w_query,
    w_key,
    w_value,
    w_out,
    final_gain,
    lm_head,
):
    groups = lax.axis_size("fsdp")
    seq_count = lax.axis_size("seq")
    seq_index = lax.axis_index("seq")
    seq_len = text_embeds.shape[0]
    width = text_embeds.shape[1]
    columns = w_key.shape[1]
    heads_local = columns // HD
    dpiece = width // groups
    quarter = groups // seq_count
    capacity = max(2, 2 * vision_tokens.shape[0] // groups)
    last_index = lengths[0] - 1

    destination = vision_request[:, 0]
    onehot = (destination[:, None] == jnp.arange(groups, dtype=jnp.int32)[None, :]).astype(
        jnp.int32
    )
    slot_index = jnp.sum((jnp.cumsum(onehot, axis=0) - onehot) * onehot, axis=1)
    counts = jnp.sum(onehot, axis=0)

    final_text = lax.dynamic_slice_in_dim(text_embeds, last_index, 1, 0)
    last_normed = row_norm(final_text, attn_gain)
    pieces = jnp.stack(
        [
            final_text.reshape(groups, dpiece),
            last_normed.reshape(groups, dpiece),
            jnp.broadcast_to(counts.astype(jnp.bfloat16)[:, None], (groups, dpiece)),
        ],
        axis=1,
    )
    pieces_in = exchange(pieces, "fsdp")
    text_part = pieces_in[:, 0]
    normed_part = pieces_in[:, 1]
    arrived = pieces_in[:, 2, :1].astype(jnp.int32)

    query_partial = jnp.dot(normed_part, w_query, preferred_element_type=jnp.float32)
    query_mine = jnp.sum(exchange(query_partial, "fsdp"), axis=0).astype(jnp.bfloat16)
    query_all = gather_by_exchange(query_mine, "fsdp", groups)

    query_heads = query_all.astype(jnp.float32).reshape(groups, heads_local, HD)
    key_rows = w_key.astype(jnp.float32).reshape(dpiece, heads_local, HD)
    probe_part = jnp.einsum(
        "rhc,dhc->rhd", query_heads, key_rows, precision=lax.Precision.HIGHEST
    )
    probe_flat = probe_part.reshape(groups, heads_local * dpiece)
    probe_high = probe_flat.astype(jnp.bfloat16)
    probe_low = (probe_flat - probe_high.astype(jnp.float32)).astype(jnp.bfloat16)

    piece_width = vision_tokens.shape[1]
    slot_of = destination * capacity + slot_index
    outbox_select = (
        jnp.arange(groups * capacity, dtype=jnp.int32)[:, None] == slot_of[None, :]
    )
    outbox = select_rows(outbox_select, vision_tokens).reshape(groups, capacity, piece_width)
    probe_halves = jnp.stack([probe_high, probe_low], axis=1)
    bundle = jnp.concatenate([outbox, probe_halves], axis=2)
    bundle_in = exchange(bundle, "fsdp")
    received_piece = bundle_in[:, :, :piece_width].reshape(groups * capacity, piece_width)
    probe_in = (
        bundle_in[:, 0, piece_width:].astype(jnp.float32)
        + bundle_in[:, 1, piece_width:].astype(jnp.float32)
    ).reshape(groups, heads_local, dpiece)
    probe = jnp.transpose(probe_in, (1, 0, 2)).reshape(heads_local, width)
    received_all = gather_by_exchange(received_piece, "seq", seq_count)
    received = jnp.transpose(received_all, (1, 0, 2)).reshape(groups * capacity, width)
    occupied = (
        (jnp.arange(capacity, dtype=jnp.int32)[None, :] < arrived).astype(jnp.int32).reshape(-1)
    )
    ranking = jnp.cumsum(occupied) - occupied
    positions = jnp.where(occupied > 0, image_start[0] + ranking, seq_len)
    place = jnp.arange(seq_len, dtype=jnp.int32)[:, None] == positions[None, :]
    placed = select_rows(place, received.reshape(-1, width))
    replaced = jnp.any(place, axis=1, keepdims=True)
    states = jnp.where(replaced, placed, text_embeds)
    normed = row_norm(states, attn_gain)

    value_sum = jnp.dot(
        normed,
        lax.all_gather(w_value, "fsdp", axis=0, tiled=True),
        preferred_element_type=jnp.float32,
    )
    value_heads = value_sum.astype(jnp.bfloat16).reshape(seq_len, heads_local, HD)
    scores = jnp.dot(
        normed.astype(jnp.float32), probe.T, precision=lax.Precision.HIGHEST
    ).T / math.sqrt(HD)
    live_keys = jnp.arange(seq_len, dtype=jnp.int32) < lengths[0]
    scores = jnp.where(live_keys[None, :], scores, -jnp.inf)
    peak = jnp.max(scores, axis=1, keepdims=True)
    shifted = jnp.exp(scores - peak)
    weights = (shifted / jnp.sum(shifted, axis=1, keepdims=True)).astype(jnp.bfloat16)
    attended = (
        jnp.einsum("hj,jhc->hc", weights, value_heads, preferred_element_type=jnp.float32)
        .astype(jnp.bfloat16)
        .reshape(columns)
    )

    attended_seq = gather_by_exchange(attended, "fsdp", groups)
    out_rows = lax.dynamic_slice_in_dim(w_out, seq_index * columns, columns, 0)
    partial_out = jnp.dot(attended_seq, out_rows, preferred_element_type=jnp.float32)
    out_mine = lax.psum_scatter(partial_out, "seq", scatter_dimension=0, tiled=True)
    text_mine = lax.dynamic_slice_in_dim(text_part, seq_index * quarter, quarter, 0)
    residual_out = text_mine.astype(jnp.float32) + out_mine
    gain_part = lax.dynamic_slice_in_dim(final_gain, lax.axis_index("fsdp") * dpiece, dpiece, 0)
    scaled_part = (residual_out * gain_part[None, :]).astype(jnp.bfloat16)
    square_part = jnp.sum(residual_out * residual_out, axis=1, keepdims=True)
    square_high = square_part.astype(jnp.bfloat16)
    square_low = (square_part - square_high.astype(jnp.float32)).astype(jnp.bfloat16)
    payload = jnp.concatenate([scaled_part, square_high, square_low], axis=1)
    payload_all = gather_by_exchange(payload, "fsdp", groups)
    scaled_out = jnp.transpose(payload_all[:, :, :dpiece], (1, 0, 2)).reshape(quarter, width)
    square_sum = jnp.sum(
        payload_all[:, :, dpiece:].astype(jnp.float32), axis=(0, 2)
    )
    mean_square = square_sum / width
    logits = jnp.dot(scaled_out, lm_head, preferred_element_type=jnp.float32)
    local_max = jnp.max(logits, axis=1) * lax.rsqrt(mean_square + norm_epsilon)
    max_all = gather_by_exchange(local_max, "fsdp", groups)
    max_logit = jnp.max(max_all, axis=0)
    return (jnp.sqrt(mean_square), max_logit)


def solution(mesh):
    return jax.shard_map(
        local,
        mesh=mesh,
        in_specs=(
            P("fsdp", None),
            P("fsdp", "seq"),
            P("fsdp", None),
            P("fsdp"),
            P("fsdp"),
            P(),
            P("fsdp", "seq"),
            P("fsdp", "seq"),
            P("fsdp", "seq"),
            P(None, "fsdp"),
            P(),
            P(None, "fsdp"),
        ),
        out_specs=(P("seq"), P("seq")),
        check_vma=False,
    )
```

```python
import math

import jax
import jax.numpy as jnp
from jax import lax
from jax.sharding import PartitionSpec as P

HD = 128


norm_epsilon = 1e-05


def row_norm(rows, gain):
    widened = rows.astype(jnp.float32)
    return (
        widened
        * lax.rsqrt(jnp.mean(widened * widened, axis=1, keepdims=True) + norm_epsilon)
        * gain
    ).astype(jnp.bfloat16)


def exchange(rows, axis_name):
    return lax.all_to_all(rows, axis_name, split_axis=0, concat_axis=0, tiled=True)


def gather_by_exchange(piece, axis_name, count):
    spread = jnp.broadcast_to(piece[None], (count,) + piece.shape)
    return exchange(spread, axis_name)


def select_rows(selector, rows):
    return jnp.dot(
        selector.astype(jnp.bfloat16), rows, preferred_element_type=jnp.float32
    ).astype(jnp.bfloat16)


def local(
    text_embeds,
    vision_tokens,
    vision_request,
    image_start,
    lengths,
    attn_gain,
    w_query,
    w_key,
    w_value,
    w_out,
    final_gain,
    lm_head,
):
    groups = lax.axis_size("fsdp")
    seq_count = lax.axis_size("seq")
    seq_index = lax.axis_index("seq")
    seq_len = text_embeds.shape[0]
    width = text_embeds.shape[1]
    columns = w_key.shape[1]
    heads_local = columns // HD
    dpiece = width // groups
    quarter = groups // seq_count
    capacity = max(2, 2 * vision_tokens.shape[0] // groups)
    last_index = lengths[0] - 1

    destination = vision_request[:, 0]
    onehot = (destination[:, None] == jnp.arange(groups, dtype=jnp.int32)[None, :]).astype(
        jnp.int32
    )
    slot_index = jnp.sum((jnp.cumsum(onehot, axis=0) - onehot) * onehot, axis=1)
    counts = jnp.sum(onehot, axis=0)

    final_text = lax.dynamic_slice_in_dim(text_embeds, last_index, 1, 0)
    last_normed = row_norm(final_text, attn_gain)
    pieces = jnp.stack(
        [
            final_text.reshape(groups, dpiece),
            last_normed.reshape(groups, dpiece),
            jnp.broadcast_to(counts.astype(jnp.bfloat16)[:, None], (groups, dpiece)),
        ],
        axis=1,
    )
    pieces_in = exchange(pieces, "fsdp")
    text_part = pieces_in[:, 0]
    normed_part = pieces_in[:, 1]
    arrived = pieces_in[:, 2, :1].astype(jnp.int32)

    query_partial = jnp.dot(normed_part, w_query, preferred_element_type=jnp.float32)
    query_mine = jnp.sum(exchange(query_partial, "fsdp"), axis=0).astype(jnp.bfloat16)
    query_all = gather_by_exchange(query_mine, "fsdp", groups)

    query_heads = query_all.astype(jnp.float32).reshape(groups, heads_local, HD)
    key_rows = w_key.astype(jnp.float32).reshape(dpiece, heads_local, HD)
    probe_part = jnp.einsum(
        "rhc,dhc->rhd", query_heads, key_rows, precision=lax.Precision.HIGHEST
    )
    probe_flat = probe_part.reshape(groups, heads_local * dpiece)
    probe_high = probe_flat.astype(jnp.bfloat16)
    probe_low = (probe_flat - probe_high.astype(jnp.float32)).astype(jnp.bfloat16)

    piece_width = vision_tokens.shape[1]
    slot_of = destination * capacity + slot_index
    outbox_select = (
        jnp.arange(groups * capacity, dtype=jnp.int32)[:, None] == slot_of[None, :]
    )
    outbox = select_rows(outbox_select, vision_tokens).reshape(groups, capacity, piece_width)
    probe_halves = jnp.stack([probe_high, probe_low], axis=1)
    bundle = jnp.concatenate([outbox, probe_halves], axis=2)
    bundle_in = exchange(bundle, "fsdp")
    received_piece = bundle_in[:, :, :piece_width].reshape(groups * capacity, piece_width)
    probe_in = (
        bundle_in[:, 0, piece_width:].astype(jnp.float32)
        + bundle_in[:, 1, piece_width:].astype(jnp.float32)
    ).reshape(groups, heads_local, dpiece)
    probe = jnp.transpose(probe_in, (1, 0, 2)).reshape(heads_local, width)
    received_all = gather_by_exchange(received_piece, "seq", seq_count)
    received = jnp.transpose(received_all, (1, 0, 2)).reshape(groups * capacity, width)
    occupied = (
        (jnp.arange(capacity, dtype=jnp.int32)[None, :] < arrived).astype(jnp.int32).reshape(-1)
    )
    ranking = jnp.cumsum(occupied) - occupied
    positions = jnp.where(occupied > 0, image_start[0] + ranking, seq_len)
    place = jnp.arange(seq_len, dtype=jnp.int32)[:, None] == positions[None, :]
    placed = select_rows(place, received.reshape(-1, width))
    replaced = jnp.any(place, axis=1, keepdims=True)
    states = jnp.where(replaced, placed, text_embeds)
    normed = row_norm(states, attn_gain)

    value_sum = jnp.dot(
        normed,
        lax.all_gather(w_value, "fsdp", axis=0, tiled=True),
        preferred_element_type=jnp.float32,
    )
    value_heads = value_sum.astype(jnp.bfloat16).reshape(seq_len, heads_local, HD)
    scores = jnp.dot(
        normed.astype(jnp.float32), probe.T, precision=lax.Precision.HIGHEST
    ).T / math.sqrt(HD)
    live_keys = jnp.arange(seq_len, dtype=jnp.int32) < lengths[0]
    scores = jnp.where(live_keys[None, :], scores, -jnp.inf)
    peak = jnp.max(scores, axis=1, keepdims=True)
    shifted = jnp.exp(scores - peak)
    weights = (shifted / jnp.sum(shifted, axis=1, keepdims=True)).astype(jnp.bfloat16)
    attended = (
        jnp.einsum("hj,jhc->hc", weights, value_heads, preferred_element_type=jnp.float32)
        .astype(jnp.bfloat16)
        .reshape(columns)
    )

    attended_every = gather_by_exchange(attended, ("fsdp", "seq"), groups * seq_count)
    attended_mine = lax.dynamic_slice_in_dim(
        attended_every.reshape(groups, seq_count * columns), seq_index * quarter, quarter, 0
    )
    out_mine = jnp.dot(attended_mine, w_out, preferred_element_type=jnp.float32)
    text_mine = lax.dynamic_slice_in_dim(text_part, seq_index * quarter, quarter, 0)
    residual_out = text_mine.astype(jnp.float32) + out_mine
    gain_part = lax.dynamic_slice_in_dim(final_gain, lax.axis_index("fsdp") * dpiece, dpiece, 0)
    scaled_part = (residual_out * gain_part[None, :]).astype(jnp.bfloat16)
    square_part = jnp.sum(residual_out * residual_out, axis=1, keepdims=True)
    square_high = square_part.astype(jnp.bfloat16)
    square_low = (square_part - square_high.astype(jnp.float32)).astype(jnp.bfloat16)
    payload = jnp.concatenate([scaled_part, square_high, square_low], axis=1)
    payload_all = gather_by_exchange(payload, "fsdp", groups)
    scaled_out = jnp.transpose(payload_all[:, :, :dpiece], (1, 0, 2)).reshape(quarter, width)
    square_sum = jnp.sum(
        payload_all[:, :, dpiece:].astype(jnp.float32), axis=(0, 2)
    )
    mean_square = square_sum / width
    logits = jnp.dot(scaled_out, lm_head, preferred_element_type=jnp.float32)
    local_max = jnp.max(logits, axis=1) * lax.rsqrt(mean_square + norm_epsilon)
    max_all = gather_by_exchange(local_max, "fsdp", groups)
    max_logit = jnp.max(max_all, axis=0)
    return (jnp.sqrt(mean_square), max_logit)


def solution(mesh):
    return jax.shard_map(
        local,
        mesh=mesh,
        in_specs=(
            P("fsdp", None),
            P("fsdp", "seq"),
            P("fsdp", None),
            P("fsdp"),
            P("fsdp"),
            P(),
            P("fsdp", "seq"),
            P("fsdp", "seq"),
            P("fsdp", "seq"),
            P(None, "fsdp"),
            P(),
            P(None, "fsdp"),
        ),
        out_specs=(P("seq"), P("seq")),
        check_vma=False,
    )
```

```python
import math

import jax
import jax.numpy as jnp
from jax import lax
from jax.sharding import PartitionSpec as P

HD = 128


norm_epsilon = 1e-05


def row_norm(rows, gain):
    widened = rows.astype(jnp.float32)
    return (
        widened
        * lax.rsqrt(jnp.mean(widened * widened, axis=1, keepdims=True) + norm_epsilon)
        * gain
    ).astype(jnp.bfloat16)


def exchange(rows, axis_name):
    return lax.all_to_all(rows, axis_name, split_axis=0, concat_axis=0, tiled=True)


def gather_by_exchange(piece, axis_name, count):
    spread = jnp.broadcast_to(piece[None], (count,) + piece.shape)
    return exchange(spread, axis_name)


def select_rows(selector, rows):
    return jnp.dot(
        selector.astype(jnp.bfloat16), rows, preferred_element_type=jnp.float32
    ).astype(jnp.bfloat16)


def local(
    text_embeds,
    vision_tokens,
    vision_request,
    image_start,
    lengths,
    attn_gain,
    w_query,
    w_key,
    w_value,
    w_out,
    final_gain,
    lm_head,
):
    groups = lax.axis_size("fsdp")
    seq_count = lax.axis_size("seq")
    seq_index = lax.axis_index("seq")
    seq_len = text_embeds.shape[0]
    width = text_embeds.shape[1]
    columns = w_key.shape[1]
    heads_local = columns // HD
    dpiece = width // groups
    quarter = groups // seq_count
    capacity = max(2, 2 * vision_tokens.shape[0] // groups)
    last_index = lengths[0] - 1

    destination = vision_request[:, 0]
    onehot = (destination[:, None] == jnp.arange(groups, dtype=jnp.int32)[None, :]).astype(
        jnp.int32
    )
    slot_index = jnp.sum((jnp.cumsum(onehot, axis=0) - onehot) * onehot, axis=1)
    counts = jnp.sum(onehot, axis=0)

    final_text = lax.dynamic_slice_in_dim(text_embeds, last_index, 1, 0)
    last_normed = row_norm(final_text, attn_gain)
    pieces_in = exchange(last_normed.reshape(groups, dpiece), "fsdp")
    normed_part = pieces_in

    query_partial = jnp.dot(normed_part, w_query, preferred_element_type=jnp.float32)
    query_mine = jnp.sum(exchange(query_partial, "fsdp"), axis=0).astype(jnp.bfloat16)
    query_all = gather_by_exchange(query_mine, "fsdp", groups)

    query_heads = query_all.astype(jnp.float32).reshape(groups, heads_local, HD)
    key_rows = w_key.astype(jnp.float32).reshape(dpiece, heads_local, HD)
    probe_part = jnp.einsum(
        "rhc,dhc->rhd", query_heads, key_rows, precision=lax.Precision.HIGHEST
    )
    probe_flat = probe_part.reshape(groups, heads_local * dpiece)
    probe_high = probe_flat.astype(jnp.bfloat16)
    probe_low = (probe_flat - probe_high.astype(jnp.float32)).astype(jnp.bfloat16)

    piece_width = vision_tokens.shape[1]
    slot_of = destination * capacity + slot_index
    outbox_select = (
        jnp.arange(groups * capacity, dtype=jnp.int32)[:, None] == slot_of[None, :]
    )
    outbox = select_rows(outbox_select, vision_tokens).reshape(groups, capacity, piece_width)
    side_high = jnp.concatenate(
        [
            probe_high,
            final_text.reshape(groups, dpiece),
            jnp.broadcast_to(counts.astype(jnp.bfloat16)[:, None], (groups, dpiece)),
            jnp.zeros((groups, probe_high.shape[1] - 2 * dpiece), jnp.bfloat16),
        ],
        axis=1,
    )
    side_low = jnp.concatenate([probe_low, jnp.zeros_like(probe_low)], axis=1)
    probe_halves = jnp.stack([side_high, side_low], axis=1)
    bundle = jnp.concatenate([outbox, probe_halves], axis=2)
    bundle_in = exchange(bundle, "fsdp")
    received_piece = bundle_in[:, :, :piece_width].reshape(groups * capacity, piece_width)
    probe_size = heads_local * dpiece
    side_start = piece_width + probe_size
    text_part = bundle_in[:, 0, side_start : side_start + dpiece]
    arrived = bundle_in[:, 0, side_start + dpiece : side_start + dpiece + 1].astype(jnp.int32)
    probe_in = (
        bundle_in[:, 0, piece_width:side_start].astype(jnp.float32)
        + bundle_in[:, 1, piece_width:side_start].astype(jnp.float32)
    ).reshape(groups, heads_local, dpiece)
    probe = jnp.transpose(probe_in, (1, 0, 2)).reshape(heads_local, width)
    received_all = gather_by_exchange(received_piece, "seq", seq_count)
    received = jnp.transpose(received_all, (1, 0, 2)).reshape(groups * capacity, width)
    occupied = (
        (jnp.arange(capacity, dtype=jnp.int32)[None, :] < arrived).astype(jnp.int32).reshape(-1)
    )
    ranking = jnp.cumsum(occupied) - occupied
    positions = jnp.where(occupied > 0, image_start[0] + ranking, seq_len)
    place = jnp.arange(seq_len, dtype=jnp.int32)[:, None] == positions[None, :]
    placed = select_rows(place, received.reshape(-1, width))
    replaced = jnp.any(place, axis=1, keepdims=True)
    states = jnp.where(replaced, placed, text_embeds)
    normed = row_norm(states, attn_gain)

    value_sum = jnp.dot(
        normed,
        lax.all_gather(w_value, "fsdp", axis=0, tiled=True),
        preferred_element_type=jnp.float32,
    )
    value_heads = value_sum.astype(jnp.bfloat16).reshape(seq_len, heads_local, HD)
    scores = jnp.dot(
        normed.astype(jnp.float32), probe.T, precision=lax.Precision.HIGHEST
    ).T / math.sqrt(HD)
    live_keys = jnp.arange(seq_len, dtype=jnp.int32) < lengths[0]
    scores = jnp.where(live_keys[None, :], scores, -jnp.inf)
    peak = jnp.max(scores, axis=1, keepdims=True)
    shifted = jnp.exp(scores - peak)
    weights = (shifted / jnp.sum(shifted, axis=1, keepdims=True)).astype(jnp.bfloat16)
    attended = (
        jnp.einsum("hj,jhc->hc", weights, value_heads, preferred_element_type=jnp.float32)
        .astype(jnp.bfloat16)
        .reshape(columns)
    )

    attended_seq = gather_by_exchange(attended, "fsdp", groups)
    out_rows = lax.dynamic_slice_in_dim(w_out, seq_index * columns, columns, 0)
    partial_out = jnp.dot(attended_seq, out_rows, preferred_element_type=jnp.float32)
    out_mine = lax.psum_scatter(partial_out, "seq", scatter_dimension=0, tiled=True)
    text_mine = lax.dynamic_slice_in_dim(text_part, seq_index * quarter, quarter, 0)
    residual_out = text_mine.astype(jnp.float32) + out_mine
    gain_part = lax.dynamic_slice_in_dim(final_gain, lax.axis_index("fsdp") * dpiece, dpiece, 0)
    scaled_part = (residual_out * gain_part[None, :]).astype(jnp.bfloat16)
    square_part = jnp.sum(residual_out * residual_out, axis=1, keepdims=True)
    square_high = square_part.astype(jnp.bfloat16)
    square_low = (square_part - square_high.astype(jnp.float32)).astype(jnp.bfloat16)
    payload = jnp.concatenate([scaled_part, square_high, square_low], axis=1)
    payload_all = gather_by_exchange(payload, "fsdp", groups)
    scaled_out = jnp.transpose(payload_all[:, :, :dpiece], (1, 0, 2)).reshape(quarter, width)
    square_sum = jnp.sum(
        payload_all[:, :, dpiece:].astype(jnp.float32), axis=(0, 2)
    )
    mean_square = square_sum / width
    logits = jnp.dot(scaled_out, lm_head, preferred_element_type=jnp.float32)
    local_max = jnp.max(logits, axis=1) * lax.rsqrt(mean_square + norm_epsilon)
    max_all = gather_by_exchange(local_max, "fsdp", groups)
    max_logit = jnp.max(max_all, axis=0)
    return (jnp.sqrt(mean_square), max_logit)


def solution(mesh):
    return jax.shard_map(
        local,
        mesh=mesh,
        in_specs=(
            P("fsdp", None),
            P("fsdp", "seq"),
            P("fsdp", None),
            P("fsdp"),
            P("fsdp"),
            P(),
            P("fsdp", "seq"),
            P("fsdp", "seq"),
            P("fsdp", "seq"),
            P(None, "fsdp"),
            P(),
            P(None, "fsdp"),
        ),
        out_specs=(P("seq"), P("seq")),
        check_vma=False,
    )
```

```python
import math

import jax
import jax.numpy as jnp
from jax import lax
from jax.sharding import PartitionSpec as P

HD = 128


norm_epsilon = 1e-05


def row_norm(rows, gain):
    widened = rows.astype(jnp.float32)
    return (
        widened
        * lax.rsqrt(jnp.mean(widened * widened, axis=1, keepdims=True) + norm_epsilon)
        * gain
    ).astype(jnp.bfloat16)


def exchange(rows, axis_name):
    return lax.all_to_all(rows, axis_name, split_axis=0, concat_axis=0, tiled=True)


def gather_by_exchange(piece, axis_name, count):
    spread = jnp.broadcast_to(piece[None], (count,) + piece.shape)
    return exchange(spread, axis_name)


def select_rows(selector, rows):
    return jnp.dot(
        selector.astype(jnp.bfloat16), rows, preferred_element_type=jnp.float32
    ).astype(jnp.bfloat16)


def local(
    text_embeds,
    vision_tokens,
    vision_request,
    image_start,
    lengths,
    attn_gain,
    w_query,
    w_key,
    w_value,
    w_out,
    final_gain,
    lm_head,
):
    groups = lax.axis_size("fsdp")
    seq_count = lax.axis_size("seq")
    seq_index = lax.axis_index("seq")
    seq_len = text_embeds.shape[0]
    width = text_embeds.shape[1]
    columns = w_key.shape[1]
    heads_local = columns // HD
    dpiece = width // groups
    quarter = groups // seq_count
    capacity = max(2, 2 * vision_tokens.shape[0] // groups)
    last_index = lengths[0] - 1

    destination = vision_request[:, 0]
    onehot = (destination[:, None] == jnp.arange(groups, dtype=jnp.int32)[None, :]).astype(
        jnp.int32
    )
    slot_index = jnp.sum((jnp.cumsum(onehot, axis=0) - onehot) * onehot, axis=1)
    counts = jnp.sum(onehot, axis=0)

    final_text = lax.dynamic_slice_in_dim(text_embeds, last_index, 1, 0)
    last_normed = row_norm(final_text, attn_gain)
    pieces = jnp.stack(
        [
            final_text.reshape(groups, dpiece),
            last_normed.reshape(groups, dpiece),
            jnp.broadcast_to(counts.astype(jnp.bfloat16)[:, None], (groups, dpiece)),
        ],
        axis=1,
    )
    pieces_in = exchange(pieces, "fsdp")
    text_part = pieces_in[:, 0]
    normed_part = pieces_in[:, 1]
    arrived = pieces_in[:, 2, :1].astype(jnp.int32)

    query_partial = jnp.dot(normed_part, w_query, preferred_element_type=jnp.float32)
    query_mine = jnp.sum(exchange(query_partial, "fsdp"), axis=0).astype(jnp.bfloat16)
    query_all = gather_by_exchange(query_mine, "fsdp", groups)

    query_heads = query_all.astype(jnp.float32).reshape(groups, heads_local, HD)
    key_rows = w_key.astype(jnp.float32).reshape(dpiece, heads_local, HD)
    probe_part = jnp.einsum(
        "rhc,dhc->rhd", query_heads, key_rows, precision=lax.Precision.HIGHEST
    )
    probe_flat = probe_part.reshape(groups, heads_local * dpiece)
    probe_high = probe_flat.astype(jnp.bfloat16)
    probe_low = (probe_flat - probe_high.astype(jnp.float32)).astype(jnp.bfloat16)

    piece_width = vision_tokens.shape[1]
    slot_of = destination * capacity + slot_index
    outbox_select = (
        jnp.arange(groups * capacity, dtype=jnp.int32)[:, None] == slot_of[None, :]
    )
    outbox = select_rows(outbox_select, vision_tokens).reshape(groups, capacity, piece_width)
    probe_halves = jnp.stack([probe_high, probe_low], axis=1)
    bundle = jnp.concatenate([outbox, probe_halves], axis=2)
    bundle_in = exchange(bundle, "fsdp")
    received_piece = bundle_in[:, :, :piece_width].reshape(groups * capacity, piece_width)
    probe_in = (
        bundle_in[:, 0, piece_width:].astype(jnp.float32)
        + bundle_in[:, 1, piece_width:].astype(jnp.float32)
    ).reshape(groups, heads_local, dpiece)
    probe = jnp.transpose(probe_in, (1, 0, 2)).reshape(heads_local, width)
    received_all = gather_by_exchange(received_piece, "seq", seq_count)
    received = jnp.transpose(received_all, (1, 0, 2)).reshape(groups * capacity, width)
    occupied = (
        (jnp.arange(capacity, dtype=jnp.int32)[None, :] < arrived).astype(jnp.int32).reshape(-1)
    )
    ranking = jnp.cumsum(occupied) - occupied
    positions = jnp.where(occupied > 0, image_start[0] + ranking, seq_len)
    place = jnp.arange(seq_len, dtype=jnp.int32)[:, None] == positions[None, :]
    placed = select_rows(place, received.reshape(-1, width))
    replaced = jnp.any(place, axis=1, keepdims=True)
    states = jnp.where(replaced, placed, text_embeds)
    normed = row_norm(states, attn_gain)

    value_sum = jnp.dot(
        normed,
        lax.all_gather(w_value, "fsdp", axis=0, tiled=True),
        preferred_element_type=jnp.float32,
    )
    value_heads = value_sum.astype(jnp.bfloat16).reshape(seq_len, heads_local, HD)
    scores = jnp.dot(
        normed.astype(jnp.float32), probe.T, precision=lax.Precision.HIGHEST
    ).T / math.sqrt(HD)
    live_keys = jnp.arange(seq_len, dtype=jnp.int32) < lengths[0]
    scores = jnp.where(live_keys[None, :], scores, -jnp.inf)
    peak = jnp.max(scores, axis=1, keepdims=True)
    shifted = jnp.exp(scores - peak)
    weights = (shifted / jnp.sum(shifted, axis=1, keepdims=True)).astype(jnp.bfloat16)
    attended = (
        jnp.einsum("hj,jhc->hc", weights, value_heads, preferred_element_type=jnp.float32)
        .astype(jnp.bfloat16)
        .reshape(columns)
    )

    attended_seq = gather_by_exchange(attended, "fsdp", groups)
    out_rows = lax.dynamic_slice_in_dim(w_out, seq_index * columns, columns, 0)
    partial_out = jnp.dot(attended_seq, out_rows, preferred_element_type=jnp.float32)
    out_mine = jnp.sum(
        exchange(partial_out.reshape(seq_count, quarter, dpiece), "seq"), axis=0
    )
    text_mine = lax.dynamic_slice_in_dim(text_part, seq_index * quarter, quarter, 0)
    residual_out = text_mine.astype(jnp.float32) + out_mine
    gain_part = lax.dynamic_slice_in_dim(final_gain, lax.axis_index("fsdp") * dpiece, dpiece, 0)
    scaled_part = (residual_out * gain_part[None, :]).astype(jnp.bfloat16)
    square_part = jnp.sum(residual_out * residual_out, axis=1, keepdims=True)
    square_high = square_part.astype(jnp.bfloat16)
    square_low = (square_part - square_high.astype(jnp.float32)).astype(jnp.bfloat16)
    payload = jnp.concatenate([scaled_part, square_high, square_low], axis=1)
    payload_all = gather_by_exchange(payload, "fsdp", groups)
    scaled_out = jnp.transpose(payload_all[:, :, :dpiece], (1, 0, 2)).reshape(quarter, width)
    square_sum = jnp.sum(
        payload_all[:, :, dpiece:].astype(jnp.float32), axis=(0, 2)
    )
    mean_square = square_sum / width
    logits = jnp.dot(scaled_out, lm_head, preferred_element_type=jnp.float32)
    local_max = jnp.max(logits, axis=1) * lax.rsqrt(mean_square + norm_epsilon)
    max_all = gather_by_exchange(local_max, "fsdp", groups)
    max_logit = jnp.max(max_all, axis=0)
    return (jnp.sqrt(mean_square), max_logit)


def solution(mesh):
    return jax.shard_map(
        local,
        mesh=mesh,
        in_specs=(
            P("fsdp", None),
            P("fsdp", "seq"),
            P("fsdp", None),
            P("fsdp"),
            P("fsdp"),
            P(),
            P("fsdp", "seq"),
            P("fsdp", "seq"),
            P("fsdp", "seq"),
            P(None, "fsdp"),
            P(),
            P(None, "fsdp"),
        ),
        out_specs=(P("seq"), P("seq")),
        check_vma=False,
    )
```
